256 devices in a mesh: section: 16 (over z_hi, y), dp: 8 (over x, core), spatial: 2 (over z_lo).
Axes of the slice: x: 4, y: 4, z: 8 (z_hi: 4, z_lo: 2; z = z_hi * 2 + z_lo), core: 2. Of those that a mesh axis runs over, the one named last changes fastest.
Arguments:
- inbox: bfloat16 [16, 4, 8, 256, 4, 128], P('section', None, 'dp', None, 'spatial'), may hold values from -6 to 6
- fresh: bfloat16 [3, 4, 8, 256, 4, 128], P(None, None, 'dp', None, 'spatial'), may hold values from -6 to 6
- params: float32 [16, 2, 9, 256, 256], P('section', None, None, ('dp', 'spatial')), may hold values from -6 to 6
- moments: float32 [16, 2, 9, 256, 256], P('section', None, None, ('dp', 'spatial')), may hold values from -3 to 3
Outputs:
- outbox: bfloat16 [16, 4, 8, 256, 4, 128], P('section', None, 'dp', None, 'spatial')
- params_out: float32 [16, 2, 9, 256, 256], P('section', None, None, ('dp', 'spatial'))
- moments_out: float32 [16, 2, 9, 256, 256], P('section', None, None, ('dp', 'spatial'))
The draws below stay inside these ranges and needn't reach their ends.
All inputs are finite; a program needn't handle non-finite values.
Results may differ from the reference program's by a relative error of at most 0.024.
Values may be sent and summed in bfloat16 or wider, within the bound.
A program may use at most 64 MiB of HBM per device.

```python
import math
import jax
import jax.numpy as jnp
from jax import lax

C = 256
TICKS = 4
IMG_DEV = 1
ROW_DEV = 2
WCOL = 128
BLOCKS = 16
IMAGES = 8
ROWS = 4
N_DP = 8
N_SPATIAL = 2


def levels(stream_key, shape, pieces, smallest, top_value):
    def one(position, blocks):
        steps = jax.random.uniform(jax.random.fold_in(jax.random.fold_in(stream_key, 6), position), (blocks,), jnp.float32, smallest / len(pieces), top_value / len(pieces))
        return jnp.repeat(jnp.exp(steps), shape[position] // blocks).reshape((-1,) + (1,) * (len(shape) - position - 1))

    factor_of = one(*pieces[0])
    for cut in pieces[1:]:
        factor_of = factor_of * one(*cut)
    return factor_of


def centred(rng, shape, scale, limit, pieces=(), kind=jnp.bfloat16):
    values = jax.random.normal(rng, shape, jnp.float32) * scale
    if len(pieces) > 0:
        values = levels(rng, shape, pieces, -0.22, 0.18) * values
    return jnp.clip(values, min=-limit, max=limit).astype(kind)


def setup_inputs(seed: int = 0) -> dict:
    key_list = jax.random.split(jax.random.key(seed), 5)
    return {
        "inbox": centred(key_list[0], (BLOCKS, 4, IMAGES, C, ROWS, WCOL), 1.0, 6.0, ((0, 16), (2, 8), (4, 2))),
        "fresh": centred(key_list[1], (TICKS - 1, 4, IMAGES, C, ROWS, WCOL), 1.0, 6.0, ((2, 8), (4, 2))),
        "params": centred(key_list[2], (BLOCKS, 2, 9, C, C), 1.0, 6.0, ((0, 16), (3, 16)), jnp.float32),
        "moments": centred(key_list[3], (BLOCKS, 2, 9, C, C), 0.5, 3.0, ((0, 16), (3, 16)), jnp.float32),
    }


learn_rate = 0.05
momentum_decay = 0.9

def rounded(value):
    return lax.optimization_barrier(value.astype(jnp.bfloat16))

def silu_slope(value):
    sigma = jax.nn.sigmoid(value)
    return sigma * (1.0 + value * (1.0 - sigma))

def flipped(kernel):
    return jnp.swapaxes(kernel[::-1], 1, 2)

def conv_full(field, kernel):
    rows, cols = (field.shape[2], field.shape[3])
    padded = jnp.pad(field.astype(jnp.float32), ((0, 0), (0, 0), (1, 1), (1, 1)))
    weights = kernel.astype(jnp.float32)
    total = jnp.zeros((field.shape[0], kernel.shape[1], rows, cols), jnp.float32)
    for tap_row in range(3):
        for tap_col in range(3):
            window = padded[:, :, tap_row:tap_row + rows, tap_col:tap_col + cols]
            total = total + jnp.einsum('oc,ncrw->norw', weights[3 * tap_row + tap_col], window, precision=lax.Precision.HIGHEST)
    return total

def kernel_grad_full(cotangent, field):
    rows, cols = (field.shape[2], field.shape[3])
    padded = jnp.pad(field.astype(jnp.float32), ((0, 0), (0, 0), (1, 1), (1, 1)))
    grads = cotangent.astype(jnp.float32).reshape(N_DP, IMG_DEV, C, N_SPATIAL, ROW_DEV, WCOL)
    taps = []
    for tap_row in range(3):
        for tap_col in range(3):
            window = padded[:, :, tap_row:tap_row + rows, tap_col:tap_col + cols]
            window = window.reshape(N_DP, IMG_DEV, C, N_SPATIAL, ROW_DEV, WCOL)
            parts = jnp.einsum('gioshw,gicshw->gsoc', grads, window, precision=lax.Precision.HIGHEST)
            parts = lax.optimization_barrier(parts.astype(jnp.bfloat16)).astype(jnp.float32)
            taps.append(lax.optimization_barrier(jnp.sum(parts, axis=(0, 1))))
    return jnp.stack(taps)

def block_step(carried):
    message, kernels = carried
    half_one, half_two, grad_one, grad_two = (message[0], message[1], message[2], message[3])
    kernel_f, kernel_g = (kernels[0], kernels[1])
    act_one = rounded(jax.nn.silu(half_one.astype(jnp.float32)))
    prev_two = rounded(half_two.astype(jnp.float32) - conv_full(act_one, kernel_g))
    back_one = rounded(grad_one.astype(jnp.float32) + silu_slope(half_one.astype(jnp.float32)) * conv_full(grad_two, flipped(kernel_g)))
    act_two = rounded(jax.nn.silu(prev_two.astype(jnp.float32)))
    prev_one = rounded(half_one.astype(jnp.float32) - conv_full(act_two, kernel_f))
    back_two = rounded(grad_two.astype(jnp.float32) + silu_slope(prev_two.astype(jnp.float32)) * conv_full(back_one, flipped(kernel_f)))
    grad_g = kernel_grad_full(grad_two, act_one)
    grad_f = kernel_grad_full(back_one, act_two)
    sent = jnp.stack([prev_one, prev_two, back_one, back_two])
    return (sent, jnp.stack([grad_f, grad_g]))

def reference(inbox, fresh, params, moments):
    scale = 1.0 / math.sqrt(9 * C)
    message = inbox
    sent = inbox
    for tick_number in range(TICKS):
        if tick_number > 0:
            message = jnp.concatenate([sent[1:], fresh[tick_number - 1][None]], axis=0)
        kernels = (params * scale).astype(jnp.bfloat16)
        sent, grads = lax.map(block_step, (message, kernels))
        moments = momentum_decay * moments + scale * grads
        params = params - learn_rate * moments
    return (sent, params, moments)
```

```python
import math

import jax
import jax.numpy as jnp
from jax import lax
from jax.experimental import pallas as pl
from jax.experimental.pallas import tpu as pltpu
from jax.sharding import PartitionSpec as P

MESH = pl.DeviceIdType.MESH
LEARN_RATE = 0.05
MOMENTUM = 0.9
F, G = 0, 1
bf16, f32 = jnp.bfloat16, jnp.float32


def wait_for(ref, sem):
    pltpu.make_async_copy(ref, ref, sem).wait()


def slope(v):
    s = jax.nn.sigmoid(v)
    return s * (1.0 + v * (1.0 - s))


def kernel(inbox, fresh, par_in, mom_in, out, par, mom,
           msg, obuf, abuf, halo, V, gp, crecv, mrecv, fs, zrecv, kbuf,
           ag_s, ag_r, rs_s, rs_r, m_s, m_r, w_s, h_s, h_r, o_s, o_r):
    ticks = msg.shape[0]
    C = msg.shape[3]
    scale = 1.0 / math.sqrt(9 * C)
    sec = lax.axis_index("section")
    n_sec = lax.axis_size("section")
    dp = lax.axis_index("dp")
    z = lax.axis_index("spatial")
    x = dp // 2
    c = lax.rem(dp, 2)
    xp, xm, x2 = lax.rem(x + 1, 4), lax.rem(x + 3, 4), lax.rem(x + 2, 4)
    XP = {"dp": lax.rem(dp + 2, 8)}
    XM = {"dp": lax.rem(dp + 6, 8)}
    CP = {"dp": dp + 1 - 2 * c}
    ZP = {"spatial": 1 - z}
    DG = {"dp": dp + 1 - 2 * c, "spatial": 1 - z}
    UP = {"section": lax.rem(sec + 1, n_sec)}
    DOWN = {"section": lax.rem(sec + n_sec - 1, n_sec)}
    top = sec == n_sec - 1
    stays = c == z

    def rc(src, dst, ss, rs, dev):
        return pltpu.make_async_remote_copy(
            src_ref=src, dst_ref=dst, send_sem=ss, recv_sem=rs,
            device_id=dev, device_id_type=MESH)

    barrier = pltpu.get_barrier_semaphore()
    for dev in (XP, XM, CP, ZP, DG, UP, DOWN):
        pl.semaphore_signal(barrier, inc=1, device_id=dev, device_id_type=MESH)
    pl.semaphore_wait(barrier, 7)

    def row(xx, cc, zz):
        return pl.multiple_of(64 * xx + 32 * cc + 16 * zz, 16)

    def kpart(k, t, xx, zz):
        return kbuf.at[k, t, :, pl.ds(row(xx, c, zz), 16), :]

    def ag(k, t, i, xx, zz, dev):
        part = kpart(k, t, xx, zz)
        return rc(part, part, ag_s.at[k, t, i], ag_r.at[k, t, i], dev)

    def ag_own(k, t):
        return [ag(k, t, 1 + z, x, z, XP), ag(k, t, 3 + z, x, z, XM),
                ag(k, t, 0, x, z, ZP), ag(k, t, 7 + z, x, z, CP)]

    def ag_pair(k, t):
        return [ag(k, t, 2 - z, x, 1 - z, XP), ag(k, t, 4 - z, x, 1 - z, XM),
                ag(k, t, 8 - z, x, 1 - z, CP)]

    def ag_wait(k, t, i):
        wait_for(kpart(k, t, x, z), ag_r.at[k, t, i])

    def gather_0(k, t):
        kbuf[k, t, :, pl.ds(row(x, c, z), 16), :] = (par[k] * scale).astype(bf16)
        for d in ag_own(k, t):
            d.start()

    def gather_1(k, t):
        ag_wait(k, t, 0)
        for d in ag_pair(k, t):
            d.start()
        ag_wait(k, t, 1)
        ag(k, t, 5, xm, 0, XP).start()
        ag(k, t, 9, xm, 0, CP).start()
        ag_wait(k, t, 4)
        ag(k, t, 6, xp, 1, XM).start()
        ag(k, t, 12, xp, 1, CP).start()
        ag_wait(k, t, 2)
        ag(k, t, 10, xm, 1, CP).start()
        ag_wait(k, t, 3)
        ag(k, t, 11, xp, 0, CP).start()

    def gather_2(k, t):
        ag_wait(k, t, 5)
        ag(k, t, 13, x2, 0, CP).start()
        ag_wait(k, t, 6)
        ag(k, t, 14, x2, 1, CP).start()

    def gather_3(k, t):
        for i in range(7, 15):
            ag_wait(k, t, i)

    def gather_sent(k, t):
        for i in range(15):
            wait_for(kpart(k, t, x, z), ag_s.at[k, t, i])

    def gpart(k, t, xx, zz):
        return gp.at[k, t, :, pl.ds(row(xx, c, zz), 16), :]

    order = (x2, xp, xm, x)

    def reduce_0(k, t):
        for j in range(4):
            rc(gp.at[k, t, :, pl.ds(row(order[j], 1 - c, 0), 32), :],
               crecv.at[k, t, :, pl.ds(pl.multiple_of(32 * order[j], 32), 32), :],
               rs_s.at[k, t, j], rs_r.at[k, t, j], CP).start()

    def to(k, t, i, m, xx, zz, dev):
        return rc(gpart(k, t, xx, zz), mrecv.at[k, t, m], rs_s.at[k, t, i], rs_r.at[k, t, i], dev)

    def reduce_1(k, t):
        for j in range(4):
            other = crecv.at[k, t, :, pl.ds(pl.multiple_of(32 * order[j], 32), 32), :]
            wait_for(other, rs_r.at[k, t, j])
            mine = gp.at[k, t, :, pl.ds(row(order[j], c, 0), 32), :]
            mine[...] = (mine[...].astype(f32) + other[...].astype(f32)).astype(bf16)
            if j == 0:
                to(k, t, 4, 0, x2, 0, XP).start()
                to(k, t, 7, 3, x2, 1, XM).start()
            if j == 1:
                to(k, t, 5, 1, xp, 1, XP).start()
            if j == 2:
                to(k, t, 8, 4, xm, 0, XM).start()

    def reduce_2(k, t):
        for m, i, xx, zz, dev in ((0, 4, xp, 0, XP), (3, 7, xm, 1, XM)):
            got = mrecv.at[k, t, m]
            wait_for(got, rs_r.at[k, t, i])
            mine = gpart(k, t, xx, zz)
            mine[...] = (mine[...].astype(f32) + got[...].astype(f32)).astype(bf16)
            to(k, t, i + 2, m + 2, xx, zz, dev).start()

    def reduce_3(k, t):
        for i, m in ((5, 1), (8, 4), (6, 2), (9, 5)):
            wait_for(mrecv.at[k, t, m], rs_r.at[k, t, i])

        def total(zz):
            return (gpart(k, t, x, zz)[...].astype(f32)
                    + mrecv[k, t, 2 - zz].astype(f32) + mrecv[k, t, 4 + zz].astype(f32))

        theirs = gpart(k, t, x, 1 - z)
        theirs[...] = total(1 - z).astype(bf16)
        rc(theirs, zrecv.at[k, t], rs_s.at[k, t, 10], rs_r.at[k, t, 10], ZP).start()
        fs[k] = total(z)

    def reduce_4(k, t):
        wait_for(zrecv.at[k, t], rs_r.at[k, t, 10])
        grad = fs[k] + zrecv[k, t].astype(f32)
        mom[k] = MOMENTUM * mom[k] + scale * grad
        par[k] = par[k] - LEARN_RATE * mom[k]

    def reduce_sent(k, t):
        for j in range(4):
            wait_for(crecv.at[k, t, :, pl.ds(0, 32), :], rs_s.at[k, t, j])
        for i in range(4, 11):
            wait_for(zrecv.at[k, t], rs_s.at[k, t, i])

    def swap(src, dst, ss, rs):
        @pl.when(stays)
        def _():
            pltpu.make_async_copy(src, dst, rs).start()

        @pl.when(jnp.logical_not(stays))
        def _():
            rc(src, dst, ss, rs, DG).start()

    def send_down(t, m):
        return rc(obuf.at[t, m], msg.at[t + 1, m], m_s.at[t + 1, m], m_r.at[t + 1, m], DOWN)

    def emit(t, members):
        @pl.when(jnp.logical_and(t < ticks - 1, sec > 0))
        def _():
            for m in members:
                send_down(t, m).start()

        @pl.when(t == ticks - 1)
        def _():
            for m in members:
                swap(obuf.at[ticks - 1, m], out.at[m], o_s.at[m], o_r.at[m])

    w = lax.broadcasted_iota(jnp.int32, (128, C), 0)

    def put(f, r, v):
        V[f, 1, r] = v.astype(bf16)
        V[f, 0, r] = jnp.where(w == 0, 0.0, pltpu.roll(v, 1, 0)).astype(bf16)
        V[f, 2, r] = jnp.where(w == 127, 0.0, pltpu.roll(v, 127, 0)).astype(bf16)

    def window(f, a, b):
        return V[f, b, a:a + 2].reshape(256, C)

    hoff = pl.multiple_of(128 * (1 - c), 128)
    hrow = 3 * (1 - c)

    def halo_send(t, f, src):
        rc(src.at[pl.ds(hoff, 128), :], halo.at[t, f], h_s.at[t, f], h_r.at[t, f], CP).start()

    def halo_put(t, f):
        wait_for(halo.at[t, f], h_r.at[t, f])
        put(f, hrow, halo[t, f].astype(f32))

    def kernel_grads(k, t, fa, g):
        gt = g.T
        for a in range(3):
            for b in range(3):
                gp[k, t, 3 * a + b] = jnp.dot(
                    gt, window(fa, a, b), preferred_element_type=f32).astype(bf16)

    def conv(k, t, f):
        acc = jnp.zeros((256, C), f32)
        for a in range(3):
            for b in range(3):
                acc = acc + lax.dot_general(
                    window(f, a, b), kbuf[k, t, 3 * a + b], (((1,), (1,)), ((), ())),
                    preferred_element_type=f32)
        return acc

    def conv_flip(k, t, f):
        acc = jnp.zeros((256, C), f32)
        for a in range(3):
            for b in range(3):
                acc = acc + jnp.dot(
                    window(f, 2 - a, 2 - b), kbuf[k, t, 3 * a + b], preferred_element_type=f32)
        return acc

    par[...] = par_in[...]
    mom[...] = mom_in[...]
    gather_0(G, 0)
    for m in (3, 0, 1, 2):
        swap(inbox.at[m], msg.at[0, m], w_s.at[0, m], m_r.at[0, m])
    gather_0(F, 0)

    @pl.when(top)
    def _():
        for t in range(ticks - 1):
            for m in range(4):
                swap(fresh.at[t, m], msg.at[t + 1, m], w_s.at[t + 1, m], m_r.at[t + 1, m])

    V[:, :, 3 * c] = jnp.zeros((4, 3, 128, C), bf16)

    def tick(t, carry):
        wait_for(msg.at[t, 3], m_r.at[t, 3])
        halo_send(t, 1, msg.at[t, 3])
        wait_for(msg.at[t, 0], m_r.at[t, 0])
        for r in range(2):
            v = msg[t, 0, 128 * r:128 * r + 128].astype(f32)
            abuf[t, 0, 128 * r:128 * r + 128] = jax.nn.silu(v).astype(bf16)
        halo_send(t, 0, abuf.at[t, 0])
        gather_1(G, t)

        @pl.when(t > 0)
        def _():
            reduce_4(F, t - 1)
            gather_0(F, t)

        for r in range(2):
            put(0, 1 + r, abuf[t, 0, 128 * r:128 * r + 128].astype(f32))
            put(1, 1 + r, msg[t, 3, 128 * r:128 * r + 128].astype(f32))
        halo_put(t, 1)
        halo_put(t, 0)
        kernel_grads(G, t, 0, msg[t, 3])
        reduce_0(G, t)
        gather_1(F, t)
        reduce_1(G, t)
        gather_2(G, t)
        gather_3(G, t)

        wait_for(msg.at[t, 1], m_r.at[t, 1])
        prev_two = (msg[t, 1].astype(f32) - conv(G, t, 0)).astype(bf16)
        obuf[t, 1] = prev_two
        abuf[t, 1] = jax.nn.silu(prev_two.astype(f32)).astype(bf16)
        halo_send(t, 2, abuf.at[t, 1])
        wait_for(msg.at[t, 2], m_r.at[t, 2])
        back_one = (msg[t, 2].astype(f32)
                    + slope(msg[t, 0].astype(f32)) * conv_flip(G, t, 1)).astype(bf16)
        obuf[t, 2] = back_one
        halo_send(t, 3, obuf.at[t, 2])
        emit(t, (1, 2))
        gather_2(F, t)
        reduce_2(G, t)
        for r in range(2):
            put(2, 1 + r, abuf[t, 1, 128 * r:128 * r + 128].astype(f32))
            put(3, 1 + r, obuf[t, 2, 128 * r:128 * r + 128].astype(f32))
        halo_put(t, 2)
        halo_put(t, 3)
        kernel_grads(F, t, 2, obuf[t, 2])
        reduce_0(F, t)
        gather_3(F, t)
        obuf[t, 0] = (msg[t, 0].astype(f32) - conv(F, t, 2)).astype(bf16)
        obuf[t, 3] = (msg[t, 3].astype(f32)
                      + slope(obuf[t, 1].astype(f32)) * conv_flip(F, t, 3)).astype(bf16)
        emit(t, (3, 0))
        reduce_1(F, t)
        reduce_3(G, t)
        reduce_2(F, t)
        reduce_4(G, t)

        @pl.when(t < ticks - 1)
        def _():
            gather_0(G, t + 1)

        reduce_3(F, t)
        gather_sent(G, t)
        gather_sent(F, t)
        reduce_sent(G, t)
        for f in range(4):
            wait_for(halo.at[t, f], h_s.at[t, f])
        return carry

    lax.fori_loop(0, ticks, tick, 0)
    reduce_4(F, ticks - 1)
    for t in range(ticks):
        reduce_sent(F, t)
    for m in range(4):
        wait_for(out.at[m], o_r.at[m])

    @pl.when(jnp.logical_not(stays))
    def _():
        for m in range(4):
            wait_for(out.at[m], o_s.at[m])
            wait_for(out.at[m], w_s.at[0, m])

    @pl.when(jnp.logical_and(top, jnp.logical_not(stays)))
    def _():
        for t in range(1, ticks):
            for m in range(4):
                wait_for(out.at[m], w_s.at[t, m])

    @pl.when(sec > 0)
    def _():
        for t in range(1, ticks):
            for m in range(4):
                wait_for(out.at[m], m_s.at[t, m])


def local(inbox, fresh, params, moments):
    T = fresh.shape[0] + 1
    C = inbox.shape[3]
    cells = inbox.shape[4] * inbox.shape[5]
    mine = inbox[0, :, 0].transpose(0, 2, 3, 1).reshape(4, cells, C)
    later = fresh[:, :, 0].transpose(0, 1, 3, 4, 2).reshape(T - 1, 4, cells, C)
    shard = params.shape[1:]
    vmem = pl.BlockSpec(memory_space=pltpu.VMEM)
    dma = pltpu.SemaphoreType.DMA
    out, par, mom = pl.pallas_call(
        kernel,
        out_shape=(jax.ShapeDtypeStruct((4, cells, C), bf16),
                   jax.ShapeDtypeStruct(shard, f32), jax.ShapeDtypeStruct(shard, f32)),
        in_specs=[vmem] * 4,
        out_specs=(vmem,) * 3,
        scratch_shapes=[
            pltpu.VMEM((T, 4, cells, C), bf16),
            pltpu.VMEM((T, 4, cells, C), bf16),
            pltpu.VMEM((T, 2, cells, C), bf16),
            pltpu.VMEM((T, 4, 128, C), bf16),
            pltpu.VMEM((4, 3, 4, 128, C), bf16),
            pltpu.VMEM((2, T, 9, C, C), bf16),
            pltpu.VMEM((2, T, 9, C // 2, C), bf16),
            pltpu.VMEM((2, T, 6, 9, 16, C), bf16),
            pltpu.VMEM((2, 9, 16, C), f32),
            pltpu.VMEM((2, T, 9, 16, C), bf16),
            pltpu.VMEM((2, T, 9, C, C), bf16),
            dma((2, T, 15)), dma((2, T, 15)),
            dma((2, T, 11)), dma((2, T, 11)),
            dma((T, 4)), dma((T, 4)), dma((T, 4)),
            dma((T, 4)), dma((T, 4)),
            dma((4,)), dma((4,)),
        ],
        compiler_params=pltpu.CompilerParams(
            collective_id=0, has_side_effects=True, vmem_limit_bytes=60 << 20),
        cost_estimate=pl.CostEstimate(
            flops=T * 6 * 9 * 2 * C * C * cells, bytes_accessed=1 << 22, transcendentals=0),
        name="relay",
    )(mine, later, params[0], moments[0])
    outbox = out.reshape(4, *inbox.shape[4:], C).transpose(0, 3, 1, 2)[None, :, None]
    return (outbox, par[None], mom[None])


def solution(mesh):
    cells = P("section", None, "dp", None, "spatial", None)
    shards = P("section", None, None, ("dp", "spatial"), None)
    return jax.shard_map(
        local,
        mesh=mesh,
        in_specs=(cells, P(None, None, "dp", None, "spatial", None), shards, shards),
        out_specs=(cells, shards, shards),
        check_vma=False,
    )
```

```python
import math

import jax
import jax.numpy as jnp
from jax import lax
from jax.experimental import pallas as pl
from jax.experimental.pallas import tpu as pltpu
from jax.sharding import PartitionSpec as P

MESH = pl.DeviceIdType.MESH
LEARN_RATE = 0.05
MOMENTUM = 0.9
F, G = 0, 1
bf16, f32 = jnp.bfloat16, jnp.float32


def wait_for(ref, sem):
    pltpu.make_async_copy(ref, ref, sem).wait()


def slope(v):
    s = jax.nn.sigmoid(v)
    return s * (1.0 + v * (1.0 - s))


def kernel(inbox, fresh, par_in, mom_in, out, par, mom,
           msg, obuf, abuf, rbuf, halo, V, gp, crecv, mrecv, fs, zrecv, kbuf,
           ag_s, ag_r, rs_s, rs_r, m_s, m_r, w_s, r_s, r_r, h_s, h_r, o_s, o_r):
    ticks = msg.shape[0]
    C = msg.shape[3]
    scale = 1.0 / math.sqrt(9 * C)
    sec = lax.axis_index("section")
    n_sec = lax.axis_size("section")
    dp = lax.axis_index("dp")
    z = lax.axis_index("spatial")
    x = dp // 2
    c = lax.rem(dp, 2)
    xp, xm, x2 = lax.rem(x + 1, 4), lax.rem(x + 3, 4), lax.rem(x + 2, 4)
    XP = {"dp": lax.rem(dp + 2, 8)}
    XM = {"dp": lax.rem(dp + 6, 8)}
    CP = {"dp": dp + 1 - 2 * c}
    ZP = {"spatial": 1 - z}
    DG = {"dp": dp + 1 - 2 * c, "spatial": 1 - z}
    def at(offset):
        return {"section": lax.rem(sec + n_sec + offset, n_sec)}

    around = jnp.logical_and(lax.rem(sec, 4) == 0, sec > 0)
    passes = jnp.logical_and(lax.rem(sec, 4) == 3, sec > 3)
    top = sec == n_sec - 1
    stays = c == z

    def rc(src, dst, ss, rs, dev):
        return pltpu.make_async_remote_copy(
            src_ref=src, dst_ref=dst, send_sem=ss, recv_sem=rs,
            device_id=dev, device_id_type=MESH)

    barrier = pltpu.get_barrier_semaphore()
    for dev in (XP, XM, CP, ZP, DG, at(1), at(-1), at(3), at(-3), at(4), at(-4)):
        pl.semaphore_signal(barrier, inc=1, device_id=dev, device_id_type=MESH)
    pl.semaphore_wait(barrier, 11)

    def row(xx, cc, zz):
        return pl.multiple_of(64 * xx + 32 * cc + 16 * zz, 16)

    def kpart(k, t, xx, zz):
        return kbuf.at[k, t, :, pl.ds(row(xx, c, zz), 16), :]

    def ag(k, t, i, xx, zz, dev):
        part = kpart(k, t, xx, zz)
        return rc(part, part, ag_s.at[k, t, i], ag_r.at[k, t, i], dev)

    def ag_own(k, t):
        return [ag(k, t, 1 + z, x, z, XP), ag(k, t, 3 + z, x, z, XM),
                ag(k, t, 0, x, z, ZP), ag(k, t, 7 + z, x, z, CP)]

    def ag_pair(k, t):
        return [ag(k, t, 2 - z, x, 1 - z, XP), ag(k, t, 4 - z, x, 1 - z, XM),
                ag(k, t, 8 - z, x, 1 - z, CP)]

    def ag_wait(k, t, i):
        wait_for(kpart(k, t, x, z), ag_r.at[k, t, i])

    def gather_0(k, t):
        kbuf[k, t, :, pl.ds(row(x, c, z), 16), :] = (par[k] * scale).astype(bf16)
        for d in ag_own(k, t):
            d.start()

    def gather_1(k, t):
        ag_wait(k, t, 0)
        for d in ag_pair(k, t):
            d.start()

    def gather_2(k, t):
        ag_wait(k, t, 1)
        ag(k, t, 5, xm, 0, XP).start()
        ag(k, t, 9, xm, 0, CP).start()
        ag_wait(k, t, 4)
        ag(k, t, 6, xp, 1, XM).start()
        ag(k, t, 12, xp, 1, CP).start()
        ag_wait(k, t, 2)
        ag(k, t, 10, xm, 1, CP).start()
        ag_wait(k, t, 3)
        ag(k, t, 11, xp, 0, CP).start()

    def gather_3(k, t):
        ag_wait(k, t, 5)
        ag(k, t, 13, x2, 0, CP).start()
        ag_wait(k, t, 6)
        ag(k, t, 14, x2, 1, CP).start()

    def gather_4(k, t):
        for i in range(7, 15):
            ag_wait(k, t, i)

    def gather_sent(k, t):
        for i in range(15):
            wait_for(kpart(k, t, x, z), ag_s.at[k, t, i])

    def gpart(k, t, xx, zz):
        return gp.at[k, t, :, pl.ds(row(xx, c, zz), 16), :]

    order = (x2, xp, xm, x)

    def reduce_0(k, t):
        for j in range(4):
            rc(gp.at[k, t, :, pl.ds(row(order[j], 1 - c, 0), 32), :],
               crecv.at[k, t, :, pl.ds(pl.multiple_of(32 * order[j], 32), 32), :],
               rs_s.at[k, t, j], rs_r.at[k, t, j], CP).start()

    def to(k, t, i, m, xx, zz, dev):
        return rc(gpart(k, t, xx, zz), mrecv.at[k, t, m], rs_s.at[k, t, i], rs_r.at[k, t, i], dev)

    def reduce_1(k, t):
        for j in range(4):
            other = crecv.at[k, t, :, pl.ds(pl.multiple_of(32 * order[j], 32), 32), :]
            wait_for(other, rs_r.at[k, t, j])
            mine = gp.at[k, t, :, pl.ds(row(order[j], c, 0), 32), :]
            mine[...] = (mine[...].astype(f32) + other[...].astype(f32)).astype(bf16)
            if j == 0:
                to(k, t, 4, 0, x2, 0, XP).start()
                to(k, t, 7, 3, x2, 1, XM).start()
            if j == 1:
                to(k, t, 5, 1, xp, 1, XP).start()
            if j == 2:
                to(k, t, 8, 4, xm, 0, XM).start()

    def reduce_2(k, t):
        for m, i, xx, zz, dev in ((0, 4, xp, 0, XP), (3, 7, xm, 1, XM)):
            got = mrecv.at[k, t, m]
            wait_for(got, rs_r.at[k, t, i])
            mine = gpart(k, t, xx, zz)
            mine[...] = (mine[...].astype(f32) + got[...].astype(f32)).astype(bf16)
            to(k, t, i + 2, m + 2, xx, zz, dev).start()

    def reduce_3(k, t):
        for i, m in ((5, 1), (8, 4), (6, 2), (9, 5)):
            wait_for(mrecv.at[k, t, m], rs_r.at[k, t, i])

        def total(zz):
            return (gpart(k, t, x, zz)[...].astype(f32)
                    + mrecv[k, t, 2 - zz].astype(f32) + mrecv[k, t, 4 + zz].astype(f32))

        theirs = gpart(k, t, x, 1 - z)
        theirs[...] = total(1 - z).astype(bf16)
        rc(theirs, zrecv.at[k, t], rs_s.at[k, t, 10], rs_r.at[k, t, 10], ZP).start()
        fs[k] = total(z)

    def reduce_4(k, t):
        wait_for(zrecv.at[k, t], rs_r.at[k, t, 10])
        grad = fs[k] + zrecv[k, t].astype(f32)
        mom[k] = MOMENTUM * mom[k] + scale * grad
        par[k] = par[k] - LEARN_RATE * mom[k]

    def reduce_sent(k, t):
        for j in range(4):
            wait_for(crecv.at[k, t, :, pl.ds(0, 32), :], rs_s.at[k, t, j])
        for i in range(4, 11):
            wait_for(zrecv.at[k, t], rs_s.at[k, t, i])

    def swap(src, dst, ss, rs):
        @pl.when(stays)
        def _():
            pltpu.make_async_copy(src, dst, rs).start()

        @pl.when(jnp.logical_not(stays))
        def _():
            rc(src, dst, ss, rs, DG).start()

    def send_down(t, m):
        return rc(obuf.at[t, m], msg.at[t + 1, m], m_s.at[t + 1, m], m_r.at[t + 1, m], at(-1))

    def send_around(t, m):
        return rc(obuf.at[t, m], rbuf.at[t, m - 1], m_s.at[t + 1, m], r_r.at[t, m - 1], at(3))

    def pass_on(t, m):
        return rc(rbuf.at[t, m - 1], msg.at[t + 1, m], r_s.at[t, m - 1], m_r.at[t + 1, m], at(-4))

    def emit_last(members):
        for m in members:
            swap(obuf.at[ticks - 1, m], out.at[m], o_s.at[m], o_r.at[m])

    def emit_early(t):
        more = t < ticks - 1

        @pl.when(jnp.logical_and(more, around))
        def _():
            for m in (1, 2):
                send_around(t, m).start()

        @pl.when(jnp.logical_and(more, lax.rem(sec, 4) > 0))
        def _():
            for m in (1, 2):
                send_down(t, m).start()

        @pl.when(jnp.logical_not(more))
        def _():
            emit_last((1, 2))

    def emit_late(t):
        more = t < ticks - 1

        @pl.when(jnp.logical_and(more, sec > 0))
        def _():
            for m in (3, 0):
                send_down(t, m).start()

        @pl.when(jnp.logical_not(more))
        def _():
            emit_last((3, 0))

    def relay(t):
        @pl.when(jnp.logical_and(t < ticks - 1, passes))
        def _():
            for m in (1, 2):
                wait_for(rbuf.at[t, m - 1], r_r.at[t, m - 1])
                pass_on(t, m).start()

    w = lax.broadcasted_iota(jnp.int32, (128, C), 0)

    def put(f, r, v):
        V[f, 1, r] = v.astype(bf16)
        V[f, 0, r] = jnp.where(w == 0, 0.0, pltpu.roll(v, 1, 0)).astype(bf16)
        V[f, 2, r] = jnp.where(w == 127, 0.0, pltpu.roll(v, 127, 0)).astype(bf16)

    def window(f, a, b):
        return V[f, b, a:a + 2].reshape(256, C)

    hoff = pl.multiple_of(128 * (1 - c), 128)
    hrow = 3 * (1 - c)

    def halo_send(t, f, src):
        rc(src.at[pl.ds(hoff, 128), :], halo.at[t, f], h_s.at[t, f], h_r.at[t, f], CP).start()

    def halo_put(t, f):
        wait_for(halo.at[t, f], h_r.at[t, f])
        put(f, hrow, halo[t, f].astype(f32))

    def kernel_grads(k, t, fa, g):
        gt = g.T
        for a in range(3):
            for b in range(3):
                gp[k, t, 3 * a + b] = jnp.dot(
                    gt, window(fa, a, b), preferred_element_type=f32).astype(bf16)

    def conv(k, t, f):
        acc = jnp.zeros((256, C), f32)
        for a in range(3):
            for b in range(3):
                acc = acc + lax.dot_general(
                    window(f, a, b), kbuf[k, t, 3 * a + b], (((1,), (1,)), ((), ())),
                    preferred_element_type=f32)
        return acc

    def conv_flip(k, t, f):
        acc = jnp.zeros((256, C), f32)
        for a in range(3):
            for b in range(3):
                acc = acc + jnp.dot(
                    window(f, 2 - a, 2 - b), kbuf[k, t, 3 * a + b], preferred_element_type=f32)
        return acc

    par[...] = par_in[...]
    mom[...] = mom_in[...]
    gather_0(G, 0)
    for m in (3, 0, 1, 2):
        swap(inbox.at[m], msg.at[0, m], w_s.at[0, m], m_r.at[0, m])
    gather_0(F, 0)

    @pl.when(top)
    def _():
        for t in range(ticks - 1):
            for m in range(4):
                swap(fresh.at[t, m], msg.at[t + 1, m], w_s.at[t + 1, m], m_r.at[t + 1, m])

    V[:, :, 3 * c] = jnp.zeros((4, 3, 128, C), bf16)
    gather_1(G, 0)

    def tick(t, carry):
        wait_for(msg.at[t, 3], m_r.at[t, 3])
        halo_send(t, 1, msg.at[t, 3])
        wait_for(msg.at[t, 0], m_r.at[t, 0])
        for r in range(2):
            v = msg[t, 0, 128 * r:128 * r + 128].astype(f32)
            abuf[t, 0, 128 * r:128 * r + 128] = jax.nn.silu(v).astype(bf16)
        halo_send(t, 0, abuf.at[t, 0])
        gather_2(G, t)
        for r in range(2):
            put(0, 1 + r, abuf[t, 0, 128 * r:128 * r + 128].astype(f32))
            put(1, 1 + r, msg[t, 3, 128 * r:128 * r + 128].astype(f32))
        halo_put(t, 1)
        halo_put(t, 0)
        kernel_grads(G, t, 0, msg[t, 3])
        reduce_0(G, t)

        @pl.when(t > 0)
        def _():
            reduce_4(F, t - 1)
            gather_0(F, t)

        gather_3(G, t)
        reduce_1(G, t)
        gather_4(G, t)

        wait_for(msg.at[t, 1], m_r.at[t, 1])
        prev_two = (msg[t, 1].astype(f32) - conv(G, t, 0)).astype(bf16)
        obuf[t, 1] = prev_two
        abuf[t, 1] = jax.nn.silu(prev_two.astype(f32)).astype(bf16)
        halo_send(t, 2, abuf.at[t, 1])
        wait_for(msg.at[t, 2], m_r.at[t, 2])
        back_one = (msg[t, 2].astype(f32)
                    + slope(msg[t, 0].astype(f32)) * conv_flip(G, t, 1)).astype(bf16)
        obuf[t, 2] = back_one
        halo_send(t, 3, obuf.at[t, 2])
        emit_early(t)
        gather_1(F, t)
        reduce_2(G, t)
        for r in range(2):
            put(2, 1 + r, abuf[t, 1, 128 * r:128 * r + 128].astype(f32))
            put(3, 1 + r, obuf[t, 2, 128 * r:128 * r + 128].astype(f32))
        halo_put(t, 2)
        halo_put(t, 3)
        kernel_grads(F, t, 2, obuf[t, 2])
        reduce_0(F, t)
        gather_2(F, t)
        reduce_3(G, t)
        reduce_1(F, t)
        gather_3(F, t)
        reduce_4(G, t)

        @pl.when(t < ticks - 1)
        def _():
            gather_0(G, t + 1)

        gather_4(F, t)
        obuf[t, 0] = (msg[t, 0].astype(f32) - conv(F, t, 2)).astype(bf16)
        obuf[t, 3] = (msg[t, 3].astype(f32)
                      + slope(obuf[t, 1].astype(f32)) * conv_flip(F, t, 3)).astype(bf16)
        emit_late(t)
        reduce_2(F, t)
        relay(t)

        @pl.when(t < ticks - 1)
        def _():
            gather_1(G, t + 1)

        reduce_3(F, t)
        gather_sent(G, t)
        gather_sent(F, t)
        reduce_sent(G, t)
        for f in range(4):
            wait_for(halo.at[t, f], h_s.at[t, f])
        return carry

    lax.fori_loop(0, ticks, tick, 0)
    reduce_4(F, ticks - 1)
    for t in range(ticks):
        reduce_sent(F, t)
    for m in range(4):
        wait_for(out.at[m], o_r.at[m])

    @pl.when(jnp.logical_not(stays))
    def _():
        for m in range(4):
            wait_for(out.at[m], o_s.at[m])
            wait_for(out.at[m], w_s.at[0, m])

    @pl.when(jnp.logical_and(top, jnp.logical_not(stays)))
    def _():
        for t in range(1, ticks):
            for m in range(4):
                wait_for(out.at[m], w_s.at[t, m])

    @pl.when(passes)
    def _():
        for t in range(ticks - 1):
            for m in range(2):
                wait_for(rbuf.at[t, m], r_s.at[t, m])

    @pl.when(sec > 0)
    def _():
        for t in range(1, ticks):
            for m in range(4):
                wait_for(out.at[m], m_s.at[t, m])


def local(inbox, fresh, params, moments):
    T = fresh.shape[0] + 1
    C = inbox.shape[3]
    cells = inbox.shape[4] * inbox.shape[5]
    mine = inbox[0, :, 0].transpose(0, 2, 3, 1).reshape(4, cells, C)
    later = fresh[:, :, 0].transpose(0, 1, 3, 4, 2).reshape(T - 1, 4, cells, C)
    shard = params.shape[1:]
    vmem = pl.BlockSpec(memory_space=pltpu.VMEM)
    dma = pltpu.SemaphoreType.DMA
    out, par, mom = pl.pallas_call(
        kernel,
        out_shape=(jax.ShapeDtypeStruct((4, cells, C), bf16),
                   jax.ShapeDtypeStruct(shard, f32), jax.ShapeDtypeStruct(shard, f32)),
        in_specs=[vmem] * 4,
        out_specs=(vmem,) * 3,
        scratch_shapes=[
            pltpu.VMEM((T, 4, cells, C), bf16),
            pltpu.VMEM((T, 4, cells, C), bf16),
            pltpu.VMEM((T, 2, cells, C), bf16),
            pltpu.VMEM((T - 1, 2, cells, C), bf16),
            pltpu.VMEM((T, 4, 128, C), bf16),
            pltpu.VMEM((4, 3, 4, 128, C), bf16),
            pltpu.VMEM((2, T, 9, C, C), bf16),
            pltpu.VMEM((2, T, 9, C // 2, C), bf16),
            pltpu.VMEM((2, T, 6, 9, 16, C), bf16),
            pltpu.VMEM((2, 9, 16, C), f32),
            pltpu.VMEM((2, T, 9, 16, C), bf16),
            pltpu.VMEM((2, T, 9, C, C), bf16),
            dma((2, T, 15)), dma((2, T, 15)),
            dma((2, T, 11)), dma((2, T, 11)),
            dma((T, 4)), dma((T, 4)), dma((T, 4)), dma((T - 1, 2)), dma((T - 1, 2)),
            dma((T, 4)), dma((T, 4)),
            dma((4,)), dma((4,)),
        ],
        compiler_params=pltpu.CompilerParams(
            collective_id=0, has_side_effects=True, vmem_limit_bytes=60 << 20),
        cost_estimate=pl.CostEstimate(
            flops=T * 6 * 9 * 2 * C * C * cells, bytes_accessed=1 << 22, transcendentals=0),
        name="relay",
    )(mine, later, params[0], moments[0])
    outbox = out.reshape(4, *inbox.shape[4:], C).transpose(0, 3, 1, 2)[None, :, None]
    return (outbox, par[None], mom[None])


def solution(mesh):
    cells = P("section", None, "dp", None, "spatial", None)
    shards = P("section", None, None, ("dp", "spatial"), None)
    return jax.shard_map(
        local,
        mesh=mesh,
        in_specs=(cells, P(None, None, "dp", None, "spatial", None), shards, shards),
        out_specs=(cells, shards, shards),
        check_vma=False,
    )
```

```python
import math

import jax
import jax.numpy as jnp
from jax import lax
from jax.experimental import pallas as pl
from jax.experimental.pallas import tpu as pltpu
from jax.sharding import PartitionSpec as P

MESH = pl.DeviceIdType.MESH
LEARN_RATE = 0.05
MOMENTUM = 0.9
F, G = 0, 1
RS = ('zf', 'zf')
AG = ('dz', 'dz')
ORDER = ('MG', 'GR', 'A1F', 'A2G', 'R1G', 'A3G', 'CG', 'A2F', 'FR', 'R2G', 'R1F', 'A3F', 'RZG', 'A0G',
         'RE', 'CF', 'R2F', 'A1G', 'FU', 'RZF', 'A0F', 'SE')
bf16, f32 = jnp.bfloat16, jnp.float32


def wait_for(ref, sem):
    pltpu.make_async_copy(ref, ref, sem).wait()


def slope(v):
    s = jax.nn.sigmoid(v)
    return s * (1.0 + v * (1.0 - s))


def kernel(inbox, fresh, par_in, mom_in, out, par, mom, last,
           msg, obuf, abuf, rbuf, halo, V, gp, crecv, mrecv, fs, kbuf, first, later, final, wide,
           ag_s, ag_r, rs_s, rs_r, m_s, m_r, f_s, f_r, r_s, r_r, h_s, h_r, o_s, o_r):
    ticks = msg.shape[0]
    C = msg.shape[3]
    scale = 1.0 / math.sqrt(9 * C)
    sec = lax.axis_index("section")
    n_sec = lax.axis_size("section")
    dp = lax.axis_index("dp")
    z = lax.axis_index("spatial")
    x = dp // 2
    c = lax.rem(dp, 2)
    xp, xm, x2 = lax.rem(x + 1, 4), lax.rem(x + 3, 4), lax.rem(x + 2, 4)
    XP = {"dp": lax.rem(dp + 2, 8)}
    XM = {"dp": lax.rem(dp + 6, 8)}
    X2 = {"dp": lax.rem(dp + 4, 8)}
    CP = {"dp": dp + 1 - 2 * c}
    ZP = {"spatial": 1 - z}
    DG = {"dp": dp + 1 - 2 * c, "spatial": 1 - z}
    def far(dev):
        return {**dev, "spatial": 1 - z}

    def at(offset):
        return {"section": lax.rem(sec + n_sec + offset, n_sec)}

    around = jnp.logical_and(lax.rem(sec, 4) == 0, sec > 0)
    passes = jnp.logical_and(lax.rem(sec, 4) == 3, sec > 3)
    top = sec == n_sec - 1
    stays = c == z

    def rc(src, dst, ss, rs, dev):
        return pltpu.make_async_remote_copy(
            src_ref=src, dst_ref=dst, send_sem=ss, recv_sem=rs,
            device_id=dev, device_id_type=MESH)

    barrier = pltpu.get_barrier_semaphore()
    for dev in (XP, XM, X2, CP, ZP, DG, far(XP), far(XM), far(X2), at(1), at(-1), at(3), at(-3), at(4), at(-4)):
        pl.semaphore_signal(barrier, inc=1, device_id=dev, device_id_type=MESH)
    pl.semaphore_wait(barrier, 15)

    def row(xx, cc, zz):
        return pl.multiple_of(64 * xx + 32 * cc + 16 * zz, 16)

    def kpart(k, t, xx, zz):
        return kbuf.at[k, t, :, pl.ds(row(xx, c, zz), 16), :]

    def ag(k, t, i, xx, zz, dev):
        part = kpart(k, t, xx, zz)
        return rc(part, part, ag_s.at[k, t, i], ag_r.at[k, t, i], dev)

    def ag_to(k, t, zz):
        ways = [ag(k, t, 5 + zz, x, zz, XP), ag(k, t, 1 + zz, x, zz, XM)]
        if AG[k] == 'dz':
            ways.append(ag(k, t, 3 + zz, x, zz, X2))
        return ways + [ag(k, t, 13 + zz, x, zz, CP)]

    def ag_wait(k, t, i):
        wait_for(kpart(k, t, x, z), ag_r.at[k, t, i])

    def gather_0(k, t):
        kbuf[k, t, :, pl.ds(row(x, c, z), 16), :] = (par[k] * scale).astype(bf16)
        ag(k, t, 0, x, z, ZP).start()
        for d in ag_to(k, t, z):
            d.start()

    def gather_1(k, t):
        ag_wait(k, t, 0)
        for d in ag_to(k, t, 1 - z):
            d.start()

    def hand_over(k, t, zz):
        for d, xx in ((0, xp), (2, xm), (1, x2)):
            ag_wait(k, t, 1 + 2 * d + zz)
            ag(k, t, 7 + 2 * d + zz, xx, zz, CP).start()

    def gather_2(k, t):
        if AG[k] == 'dz':
            hand_over(k, t, z)
            return
        ag_wait(k, t, 5)
        ag(k, t, 3, xm, 0, XP).start()
        ag(k, t, 11, xm, 0, CP).start()
        ag_wait(k, t, 2)
        ag(k, t, 4, xp, 1, XM).start()
        ag(k, t, 8, xp, 1, CP).start()
        ag_wait(k, t, 6)
        ag(k, t, 12, xm, 1, CP).start()
        ag_wait(k, t, 1)
        ag(k, t, 7, xp, 0, CP).start()

    def gather_3(k, t):
        if AG[k] == 'dz':
            hand_over(k, t, 1 - z)
            return
        for zz in range(2):
            ag_wait(k, t, 3 + zz)
            ag(k, t, 9 + zz, x2, zz, CP).start()

    def gather_4(k, t):
        for i in range(7, 15):
            ag_wait(k, t, i)

    def gather_sent(k, t):
        for i in range(15):
            wait_for(kpart(k, t, x, z), ag_s.at[k, t, i])

    def gpart(k, t, xx, zz):
        return gp.at[k, t, :, pl.ds(row(xx, c, zz), 16), :]

    order = (x2, xp, xm, x)

    def reduce_0(k, t):
        for j in range(4):
            rc(gp.at[k, t, :, pl.ds(row(order[j], 1 - c, 0), 32), :],
               crecv.at[k, t, :, pl.ds(pl.multiple_of(32 * order[j], 32), 32), :],
               rs_s.at[k, t, j], rs_r.at[k, t, j], CP).start()

    def part_to(k, t, m, xx, zz, dev):
        return rc(gpart(k, t, xx, zz), mrecv.at[k, t, m], rs_s.at[k, t, 4 + m], rs_r.at[k, t, 4 + m], dev)

    def part_wait(k, t, m):
        wait_for(mrecv.at[k, t, m], rs_r.at[k, t, 4 + m])

    def part_add(k, t, m, xx, zz):
        part_wait(k, t, m)
        mine = gpart(k, t, xx, zz)
        mine[...] = (mine[...].astype(f32) + mrecv[k, t, m].astype(f32)).astype(bf16)

    def reduce_1(k, t):
        for j in range(4):
            xx = order[j]
            other = crecv.at[k, t, :, pl.ds(pl.multiple_of(32 * xx, 32), 32), :]
            wait_for(other, rs_r.at[k, t, j])
            mine = gp.at[k, t, :, pl.ds(row(xx, c, 0), 32), :]
            mine[...] = (mine[...].astype(f32) + other[...].astype(f32)).astype(bf16)
            dev = (X2, XP, XM, None)[j]
            m = (2, 0, 1, 6)[j]
            if RS[k] == 'zf':
                part_to(k, t, j, xx, 1 - z, ZP).start()
            elif RS[k] == 'cur':
                if j == 0:
                    part_to(k, t, 0, xx, 0, XP).start()
                    part_to(k, t, 3, xx, 1, XM).start()
                elif j == 1:
                    part_to(k, t, 1, xx, 1, XP).start()
                elif j == 2:
                    part_to(k, t, 4, xx, 0, XM).start()
            elif dev is None:
                part_to(k, t, 6, xx, 1 - z, ZP).start()
            else:
                part_to(k, t, m + 3, xx, 1 - z, far(dev)).start()
                part_to(k, t, m, xx, z, dev).start()

    def reduce_2(k, t):
        if RS[k] == 'zf':
            for j in range(4):
                part_add(k, t, j, order[j], z)
                if j < 3:
                    part_to(k, t, 4 + j, order[j], z, (X2, XP, XM)[j]).start()
        if RS[k] == 'cur':
            part_add(k, t, 0, xp, 0)
            part_to(k, t, 2, xp, 0, XP).start()
            part_add(k, t, 3, xm, 1)
            part_to(k, t, 5, xm, 1, XM).start()

    def reduce_3(k, t):
        if RS[k] == 'cur':
            for m in (1, 4, 2, 5):
                part_wait(k, t, m)

            def total(zz):
                return (gpart(k, t, x, zz)[...].astype(f32)
                        + mrecv[k, t, 2 - zz].astype(f32) + mrecv[k, t, 4 + zz].astype(f32))

            theirs = gpart(k, t, x, 1 - z)
            theirs[...] = total(1 - z).astype(bf16)
            part_to(k, t, 6, x, 1 - z, ZP).start()
            fs[k] = total(z)

    def update(k, t):
        late = {'zf': (4, 5, 6), 'cur': (6,), 'direct': range(7)}[RS[k]]
        grad = fs[k] if RS[k] == 'cur' else gpart(k, t, x, z)[...].astype(f32)
        for m in late:
            part_wait(k, t, m)
        for m in late:
            grad = grad + mrecv[k, t, m].astype(f32)
        @pl.when(t < ticks - 1)
        def _():
            mom[k] = MOMENTUM * mom[k] + scale * grad
            par[k] = par[k] - LEARN_RATE * mom[k]

        @pl.when(t == ticks - 1)
        def _():
            last[k] = grad

    def reduce_sent(k, t):
        for j in range(4):
            wait_for(crecv.at[k, t, :, pl.ds(0, 32), :], rs_s.at[k, t, j])
        for i in range(4, 11):
            wait_for(mrecv.at[k, t, 0], rs_s.at[k, t, i])

    def swap(src, dst, ss, rs):
        @pl.when(stays)
        def _():
            pltpu.make_async_copy(src, dst, rs).start()

        @pl.when(jnp.logical_not(stays))
        def _():
            rc(src, dst, ss, rs, DG).start()

    def send_down(t, m):
        return rc(obuf.at[t, m], msg.at[t + 1, m], m_s.at[t + 1, m], m_r.at[t + 1, m], at(-1))

    def send_around(t, m):
        return rc(obuf.at[t, m], rbuf.at[t, m - 1], m_s.at[t + 1, m], r_r.at[t, m - 1], at(3))

    def pass_on(t, m):
        return rc(rbuf.at[t, m - 1], msg.at[t + 1, m], r_s.at[t, m - 1], m_r.at[t + 1, m], at(-4))

    def emit_last(members):
        for m in members:
            pack(obuf.at[ticks - 1, m], final.at[m])
            swap(final.at[m], out.at[m], o_s.at[m], o_r.at[m])

    def emit_early(t):
        more = t < ticks - 1

        @pl.when(jnp.logical_and(more, around))
        def _():
            for m in (1, 2):
                send_around(t, m).start()

        @pl.when(jnp.logical_and(more, lax.rem(sec, 4) > 0))
        def _():
            for m in (1, 2):
                send_down(t, m).start()

        @pl.when(jnp.logical_not(more))
        def _():
            emit_last((1, 2))

    def emit_late(t):
        more = t < ticks - 1

        @pl.when(jnp.logical_and(more, sec > 0))
        def _():
            for m in (3, 0):
                send_down(t, m).start()

        @pl.when(jnp.logical_not(more))
        def _():
            emit_last((3, 0))

    def relay(t):
        @pl.when(jnp.logical_and(t < ticks - 1, passes))
        def _():
            for m in (1, 2):
                wait_for(rbuf.at[t, m - 1], r_r.at[t, m - 1])
                pass_on(t, m).start()

    def unpack(src, dst):
        wide[...] = src[...].astype(f32)
        for r in range(2):
            dst[128 * r:128 * r + 128] = wide[pl.ds(r, C, stride=2), :].T.astype(bf16)

    def pack(src, dst):
        for r in range(2):
            wide[pl.ds(r, C, stride=2), :] = src[128 * r:128 * r + 128].astype(f32).T
        dst[...] = wide[...].astype(bf16)

    def msg_wait(t, m):
        @pl.when(jnp.logical_and(t > 0, jnp.logical_not(top)))
        def _():
            wait_for(msg.at[t, m], m_r.at[t, m])

    def take_fresh(t):
        @pl.when(jnp.logical_and(t < ticks - 1, top))
        def _():
            for m in (3, 0, 1, 2):
                wait_for(later.at[t, m], f_r.at[t + 1, m])
                unpack(later.at[t, m], msg.at[t + 1, m])

    w = lax.broadcasted_iota(jnp.int32, (128, C), 0)

    def put(f, r, v):
        V[f, 1, r] = v.astype(bf16)
        V[f, 0, r] = jnp.where(w == 0, 0.0, pltpu.roll(v, 1, 0)).astype(bf16)
        V[f, 2, r] = jnp.where(w == 127, 0.0, pltpu.roll(v, 127, 0)).astype(bf16)

    def window(f, a, b):
        return V[f, b, a:a + 2].reshape(256, C)

    hoff = pl.multiple_of(128 * (1 - c), 128)
    hrow = 3 * (1 - c)

    def halo_send(t, f, src):
        rc(src.at[pl.ds(hoff, 128), :], halo.at[t, f], h_s.at[t, f], h_r.at[t, f], CP).start()

    def halo_put(t, f):
        wait_for(halo.at[t, f], h_r.at[t, f])
        put(f, hrow, halo[t, f].astype(f32))

    def kernel_grads(k, t, fa, g):
        gt = g.T
        for a in range(3):
            for b in range(3):
                gp[k, t, 3 * a + b] = jnp.dot(
                    gt, window(fa, a, b), preferred_element_type=f32).astype(bf16)

    def conv(k, t, f):
        acc = jnp.zeros((256, C), f32)
        for a in range(3):
            for b in range(3):
                acc = acc + lax.dot_general(
                    window(f, a, b), kbuf[k, t, 3 * a + b], (((1,), (1,)), ((), ())),
                    preferred_element_type=f32)
        return acc

    def conv_flip(k, t, f):
        acc = jnp.zeros((256, C), f32)
        for a in range(3):
            for b in range(3):
                acc = acc + jnp.dot(
                    window(f, 2 - a, 2 - b), kbuf[k, t, 3 * a + b], preferred_element_type=f32)
        return acc

    par[...] = par_in[...]
    mom[...] = mom_in[...]
    gather_0(G, 0)
    for m in (3, 0, 1, 2):
        swap(inbox.at[m], first.at[m], f_s.at[0, m], f_r.at[0, m])
    gather_0(F, 0)

    @pl.when(top)
    def _():
        for t in range(ticks - 1):
            for m in (3, 0, 1, 2):
                swap(fresh.at[t, m], later.at[t, m], f_s.at[t + 1, m], f_r.at[t + 1, m])

    V[:, :, 3 * c] = jnp.zeros((4, 3, 128, C), bf16)
    def open_first(m):
        wait_for(first.at[m], f_r.at[0, m])
        unpack(first.at[m], msg.at[0, m])

    open_first(3)
    open_first(0)
    for k, name in ((G, 'A1G'), (F, 'A1F')):
        if name not in ORDER[:ORDER.index('C' + name[-1])]:
            gather_1(k, 0)
    open_first(1)
    open_first(2)

    def begin(t):
        msg_wait(t, 3)
        halo_send(t, 1, msg.at[t, 3])
        msg_wait(t, 0)
        for r in range(2):
            v = msg[t, 0, 128 * r:128 * r + 128].astype(f32)
            abuf[t, 0, 128 * r:128 * r + 128] = jax.nn.silu(v).astype(bf16)
        halo_send(t, 0, abuf.at[t, 0])
        for r in range(2):
            put(0, 1 + r, abuf[t, 0, 128 * r:128 * r + 128].astype(f32))
            put(1, 1 + r, msg[t, 3, 128 * r:128 * r + 128].astype(f32))

    def grads_g(t):
        halo_put(t, 1)
        halo_put(t, 0)
        kernel_grads(G, t, 0, msg[t, 3])
        reduce_0(G, t)

    def convs_g(t):
        gather_4(G, t)
        msg_wait(t, 1)
        prev_two = (msg[t, 1].astype(f32) - conv(G, t, 0)).astype(bf16)
        obuf[t, 1] = prev_two
        abuf[t, 1] = jax.nn.silu(prev_two.astype(f32)).astype(bf16)
        halo_send(t, 2, abuf.at[t, 1])
        msg_wait(t, 2)
        back_one = (msg[t, 2].astype(f32)
                    + slope(msg[t, 0].astype(f32)) * conv_flip(G, t, 1)).astype(bf16)
        obuf[t, 2] = back_one
        halo_send(t, 3, obuf.at[t, 2])
        emit_early(t)
        for r in range(2):
            put(2, 1 + r, abuf[t, 1, 128 * r:128 * r + 128].astype(f32))
            put(3, 1 + r, obuf[t, 2, 128 * r:128 * r + 128].astype(f32))

    def grads_f(t):
        halo_put(t, 2)
        halo_put(t, 3)
        kernel_grads(F, t, 2, obuf[t, 2])
        reduce_0(F, t)

    def convs_f(t):
        gather_4(F, t)
        obuf[t, 0] = (msg[t, 0].astype(f32) - conv(F, t, 2)).astype(bf16)
        obuf[t, 3] = (msg[t, 3].astype(f32)
                      + slope(obuf[t, 1].astype(f32)) * conv_flip(F, t, 3)).astype(bf16)
        emit_late(t)

    def sent(t):
        gather_sent(G, t)
        gather_sent(F, t)
        reduce_sent(G, t)
        reduce_sent(F, t)
        for f in range(4):
            wait_for(halo.at[t, f], h_s.at[t, f])

    def step(name, t):
        k = G if name[-1] == 'G' else F
        plain = {'MG': begin, 'GR': grads_g, 'CG': convs_g, 'FR': grads_f, 'CF': convs_f,
                 'RE': relay, 'FU': take_fresh, 'SE': sent}
        if name in plain:
            plain[name](t)
            return
        stage = {'A0': gather_0, 'A1': gather_1, 'A2': gather_2, 'A3': gather_3,
                 'R1': reduce_1, 'R2': reduce_2, 'R3': reduce_3, 'RZ': update}[name[:2]]
        if name[:2] in ('A0', 'A1') and name not in ORDER[:ORDER.index('C' + name[-1])]:
            @pl.when(t < ticks - 1)
            def _():
                stage(k, t + 1)
        else:
            stage(k, t)

    def tick(t, carry):
        for name in ORDER:
            step(name, t)
        return carry

    lax.fori_loop(0, ticks, tick, 0)
    for m in range(4):
        wait_for(out.at[m], o_r.at[m])

    @pl.when(jnp.logical_not(stays))
    def _():
        for m in range(4):
            wait_for(out.at[m], o_s.at[m])
            wait_for(out.at[m], f_s.at[0, m])

    @pl.when(jnp.logical_and(top, jnp.logical_not(stays)))
    def _():
        for t in range(1, ticks):
            for m in range(4):
                wait_for(out.at[m], f_s.at[t, m])

    @pl.when(passes)
    def _():
        for t in range(ticks - 1):
            for m in range(2):
                wait_for(rbuf.at[t, m], r_s.at[t, m])

    @pl.when(sec > 0)
    def _():
        for t in range(1, ticks):
            for m in range(4):
                wait_for(out.at[m], m_s.at[t, m])


def local(inbox, fresh, params, moments):
    T = fresh.shape[0] + 1
    C = inbox.shape[3]
    cells = inbox.shape[4] * inbox.shape[5]
    raw = (C * inbox.shape[4], inbox.shape[5])
    mine = inbox.reshape(4, *raw)
    later = fresh.reshape(T - 1, 4, *raw)
    shard = params.shape[1:]
    vmem = pl.BlockSpec(memory_space=pltpu.VMEM)
    dma = pltpu.SemaphoreType.DMA
    out, par, mom, grad = pl.pallas_call(
        kernel,
        out_shape=(jax.ShapeDtypeStruct((4, *raw), bf16),) + (jax.ShapeDtypeStruct(shard, f32),) * 3,
        in_specs=[vmem, pl.BlockSpec(memory_space=pl.ANY), vmem, vmem],
        out_specs=(vmem,) * 4,
        scratch_shapes=[
            pltpu.VMEM((T, 4, cells, C), bf16),
            pltpu.VMEM((T, 4, cells, C), bf16),
            pltpu.VMEM((T, 2, cells, C), bf16),
            pltpu.VMEM((T - 1, 2, cells, C), bf16),
            pltpu.VMEM((T, 4, 128, C), bf16),
            pltpu.VMEM((4, 3, 4, 128, C), bf16),
            pltpu.VMEM((2, T, 9, C, C), bf16),
            pltpu.VMEM((2, T, 9, C // 2, C), bf16),
            pltpu.VMEM((2, T, 7, 9, 16, C), bf16),
            pltpu.VMEM((2, 9, 16, C), f32),
            pltpu.VMEM((2, T, 9, C, C), bf16),
            pltpu.VMEM((4, *raw), bf16),
            pltpu.VMEM((T - 1, 4, *raw), bf16),
            pltpu.VMEM((4, *raw), bf16),
            pltpu.VMEM(raw, f32),
            dma((2, T, 15)), dma((2, T, 15)),
            dma((2, T, 11)), dma((2, T, 11)),
            dma((T, 4)), dma((T, 4)), dma((T, 4)), dma((T, 4)), dma((T - 1, 2)), dma((T - 1, 2)),
            dma((T, 4)), dma((T, 4)),
            dma((4,)), dma((4,)),
        ],
        compiler_params=pltpu.CompilerParams(
            collective_id=0, has_side_effects=True, vmem_limit_bytes=60 << 20),
        cost_estimate=pl.CostEstimate(
            flops=T * 6 * 9 * 2 * C * C * cells, bytes_accessed=1 << 22, transcendentals=0),
        name="relay",
    )(mine, later, params[0], moments[0])
    mom = MOMENTUM * mom + grad / math.sqrt(9 * C)
    par = par - LEARN_RATE * mom
    return (out.reshape(inbox.shape), par[None], mom[None])


def solution(mesh):
    cells = P("section", None, "dp", None, "spatial", None)
    shards = P("section", None, None, ("dp", "spatial"), None)
    return jax.shard_map(
        local,
        mesh=mesh,
        in_specs=(cells, P(None, None, "dp", None, "spatial", None), shards, shards),
        out_specs=(cells, shards, shards),
        check_vma=False,
    )
```

```python
import math

import jax
import jax.numpy as jnp
from jax import lax
from jax.experimental import pallas as pl
from jax.experimental.pallas import tpu as pltpu
from jax.sharding import PartitionSpec as P

MESH = pl.DeviceIdType.MESH
LEARN_RATE = 0.05
MOMENTUM = 0.9
F, G = 0, 1
RS = ('xf', 'zf')
AG = ('dz', 'dz')
ORDER = ('MG', 'GR', 'A1F', 'A2G', 'R1G', 'A3G', 'CG', 'A2F', 'FR', 'R2G', 'R1F', 'A3F', 'RZG', 'A0G',
         'RE', 'CF', 'R2F', 'A1G', 'FU', 'RZF', 'A0F', 'SE')
bf16, f32 = jnp.bfloat16, jnp.float32


def wait_for(ref, sem):
    pltpu.make_async_copy(ref, ref, sem).wait()


def slope(v):
    s = jax.nn.sigmoid(v)
    return s * (1.0 + v * (1.0 - s))


def kernel(inbox, fresh, par_in, mom_in, out, par, mom, last,
           msg, obuf, abuf, rbuf, halo, V, gp, crecv, mrecv, fs, kbuf, first, later, final, wide,
           ag_s, ag_r, rs_s, rs_r, m_s, m_r, f_s, f_r, r_s, r_r, h_s, h_r, o_s, o_r):
    ticks = msg.shape[0]
    C = msg.shape[3]
    scale = 1.0 / math.sqrt(9 * C)
    sec = lax.axis_index("section")
    n_sec = lax.axis_size("section")
    dp = lax.axis_index("dp")
    z = lax.axis_index("spatial")
    x = dp // 2
    c = lax.rem(dp, 2)
    xp, xm, x2 = lax.rem(x + 1, 4), lax.rem(x + 3, 4), lax.rem(x + 2, 4)
    XP = {"dp": lax.rem(dp + 2, 8)}
    XM = {"dp": lax.rem(dp + 6, 8)}
    X2 = {"dp": lax.rem(dp + 4, 8)}
    CP = {"dp": dp + 1 - 2 * c}
    ZP = {"spatial": 1 - z}
    DG = {"dp": dp + 1 - 2 * c, "spatial": 1 - z}
    def far(dev):
        return {**dev, "spatial": 1 - z}

    def at(offset):
        return {"section": lax.rem(sec + n_sec + offset, n_sec)}

    around = jnp.logical_and(lax.rem(sec, 4) == 0, sec > 0)
    passes = jnp.logical_and(lax.rem(sec, 4) == 3, sec > 3)
    top = sec == n_sec - 1
    stays = c == z

    def rc(src, dst, ss, rs, dev):
        return pltpu.make_async_remote_copy(
            src_ref=src, dst_ref=dst, send_sem=ss, recv_sem=rs,
            device_id=dev, device_id_type=MESH)

    barrier = pltpu.get_barrier_semaphore()
    for dev in (XP, XM, X2, CP, ZP, DG, far(XP), far(XM), far(X2), at(1), at(-1), at(3), at(-3), at(4), at(-4)):
        pl.semaphore_signal(barrier, inc=1, device_id=dev, device_id_type=MESH)
    pl.semaphore_wait(barrier, 15)

    def row(xx, cc, zz):
        return pl.multiple_of(64 * xx + 32 * cc + 16 * zz, 16)

    def kpart(k, t, xx, zz):
        return kbuf.at[k, t, :, pl.ds(row(xx, c, zz), 16), :]

    def ag(k, t, i, xx, zz, dev):
        part = kpart(k, t, xx, zz)
        return rc(part, part, ag_s.at[k, t, i], ag_r.at[k, t, i], dev)

    def ag_to(k, t, zz):
        ways = [ag(k, t, 5 + zz, x, zz, XP), ag(k, t, 1 + zz, x, zz, XM)]
        if AG[k] == 'dz':
            ways.append(ag(k, t, 3 + zz, x, zz, X2))
        return ways + [ag(k, t, 13 + zz, x, zz, CP)]

    def ag_wait(k, t, i):
        wait_for(kpart(k, t, x, z), ag_r.at[k, t, i])

    def gather_0(k, t):
        kbuf[k, t, :, pl.ds(row(x, c, z), 16), :] = (par[k] * scale).astype(bf16)
        ag(k, t, 0, x, z, ZP).start()
        for d in ag_to(k, t, z):
            d.start()

    def gather_1(k, t):
        ag_wait(k, t, 0)
        for d in ag_to(k, t, 1 - z):
            d.start()

    def hand_over(k, t, zz):
        for d, xx in ((0, xp), (2, xm), (1, x2)):
            ag_wait(k, t, 1 + 2 * d + zz)
            ag(k, t, 7 + 2 * d + zz, xx, zz, CP).start()

    def gather_2(k, t):
        if AG[k] == 'dz':
            hand_over(k, t, z)
            return
        ag_wait(k, t, 5)
        ag(k, t, 3, xm, 0, XP).start()
        ag(k, t, 11, xm, 0, CP).start()
        ag_wait(k, t, 2)
        ag(k, t, 4, xp, 1, XM).start()
        ag(k, t, 8, xp, 1, CP).start()
        ag_wait(k, t, 6)
        ag(k, t, 12, xm, 1, CP).start()
        ag_wait(k, t, 1)
        ag(k, t, 7, xp, 0, CP).start()

    def gather_3(k, t):
        if AG[k] == 'dz':
            hand_over(k, t, 1 - z)
            return
        for zz in range(2):
            ag_wait(k, t, 3 + zz)
            ag(k, t, 9 + zz, x2, zz, CP).start()

    def gather_4(k, t):
        for i in range(7, 15):
            ag_wait(k, t, i)

    def gather_sent(k, t):
        for i in range(15):
            wait_for(kpart(k, t, x, z), ag_s.at[k, t, i])

    def gpart(k, t, xx, zz):
        return gp.at[k, t, :, pl.ds(row(xx, c, zz), 16), :]

    order = (x2, xp, xm, x)

    def reduce_0(k, t):
        for j in range(4):
            rc(gp.at[k, t, :, pl.ds(row(order[j], 1 - c, 0), 32), :],
               crecv.at[k, t, :, pl.ds(pl.multiple_of(32 * order[j], 32), 32), :],
               rs_s.at[k, t, j], rs_r.at[k, t, j], CP).start()

    def part_to(k, t, m, xx, zz, dev):
        return rc(gpart(k, t, xx, zz), mrecv.at[k, t, m], rs_s.at[k, t, 4 + m], rs_r.at[k, t, 4 + m], dev)

    def part_wait(k, t, m):
        wait_for(mrecv.at[k, t, m], rs_r.at[k, t, 4 + m])

    def part_add(k, t, m, xx, zz):
        part_wait(k, t, m)
        mine = gpart(k, t, xx, zz)
        mine[...] = (mine[...].astype(f32) + mrecv[k, t, m].astype(f32)).astype(bf16)

    def reduce_1(k, t):
        for j in range(4):
            xx = order[j]
            other = crecv.at[k, t, :, pl.ds(pl.multiple_of(32 * xx, 32), 32), :]
            wait_for(other, rs_r.at[k, t, j])
            mine = gp.at[k, t, :, pl.ds(row(xx, c, 0), 32), :]
            mine[...] = (mine[...].astype(f32) + other[...].astype(f32)).astype(bf16)
            dev = (X2, XP, XM, None)[j]
            m = (2, 0, 1, 6)[j]
            if RS[k] == 'zf':
                part_to(k, t, j, xx, 1 - z, ZP).start()
            elif RS[k] == 'xf':
                for zz in range(2):
                    if j < 3:
                        part_to(k, t, 2 * j + zz, xx, zz, dev).start()
            elif RS[k] == 'cur':
                if j == 0:
                    part_to(k, t, 0, xx, 0, XP).start()
                    part_to(k, t, 3, xx, 1, XM).start()
                elif j == 1:
                    part_to(k, t, 1, xx, 1, XP).start()
                elif j == 2:
                    part_to(k, t, 4, xx, 0, XM).start()
            elif dev is None:
                part_to(k, t, 6, xx, 1 - z, ZP).start()
            else:
                part_to(k, t, m + 3, xx, 1 - z, far(dev)).start()
                part_to(k, t, m, xx, z, dev).start()

    def reduce_2(k, t):
        if RS[k] == 'zf':
            for j in range(4):
                part_add(k, t, j, order[j], z)
                if j < 3:
                    part_to(k, t, 4 + j, order[j], z, (X2, XP, XM)[j]).start()
        if RS[k] == 'cur':
            part_add(k, t, 0, xp, 0)
            part_to(k, t, 2, xp, 0, XP).start()
            part_add(k, t, 3, xm, 1)
            part_to(k, t, 5, xm, 1, XM).start()

        if RS[k] == 'xf':
            for m in (2, 3, 4, 5, 0, 1):
                part_wait(k, t, m)

            def total(zz):
                grad = gpart(k, t, x, zz)[...].astype(f32)
                for j in range(3):
                    grad = grad + mrecv[k, t, 2 * j + zz].astype(f32)
                return grad

            theirs = gpart(k, t, x, 1 - z)
            theirs[...] = total(1 - z).astype(bf16)
            part_to(k, t, 6, x, 1 - z, ZP).start()
            fs[k] = total(z)

    def reduce_3(k, t):
        if RS[k] == 'cur':
            for m in (1, 4, 2, 5):
                part_wait(k, t, m)

            def total(zz):
                return (gpart(k, t, x, zz)[...].astype(f32)
                        + mrecv[k, t, 2 - zz].astype(f32) + mrecv[k, t, 4 + zz].astype(f32))

            theirs = gpart(k, t, x, 1 - z)
            theirs[...] = total(1 - z).astype(bf16)
            part_to(k, t, 6, x, 1 - z, ZP).start()
            fs[k] = total(z)

    def update(k, t):
        late = {'zf': (4, 5, 6), 'cur': (6,), 'xf': (6,), 'direct': range(7)}[RS[k]]
        grad = fs[k] if RS[k] in ('cur', 'xf') else gpart(k, t, x, z)[...].astype(f32)
        for m in late:
            part_wait(k, t, m)
        for m in late:
            grad = grad + mrecv[k, t, m].astype(f32)
        @pl.when(t < ticks - 1)
        def _():
            mom[k] = MOMENTUM * mom[k] + scale * grad
            par[k] = par[k] - LEARN_RATE * mom[k]

        @pl.when(t == ticks - 1)
        def _():
            last[k] = grad

    def reduce_sent(k, t):
        for j in range(4):
            wait_for(crecv.at[k, t, :, pl.ds(0, 32), :], rs_s.at[k, t, j])
        for i in range(4, 11):
            wait_for(mrecv.at[k, t, 0], rs_s.at[k, t, i])

    def swap(src, dst, ss, rs):
        @pl.when(stays)
        def _():
            pltpu.make_async_copy(src, dst, rs).start()

        @pl.when(jnp.logical_not(stays))
        def _():
            rc(src, dst, ss, rs, DG).start()

    def send_down(t, m):
        return rc(obuf.at[t, m], msg.at[t + 1, m], m_s.at[t + 1, m], m_r.at[t + 1, m], at(-1))

    def send_around(t, m):
        return rc(obuf.at[t, m], rbuf.at[t, m - 1], m_s.at[t + 1, m], r_r.at[t, m - 1], at(3))

    def pass_on(t, m):
        return rc(rbuf.at[t, m - 1], msg.at[t + 1, m], r_s.at[t, m - 1], m_r.at[t + 1, m], at(-4))

    def emit_last(members):
        for m in members:
            pack(obuf.at[ticks - 1, m], final.at[m])
            swap(final.at[m], out.at[m], o_s.at[m], o_r.at[m])

    def emit_early(t):
        more = t < ticks - 1

        @pl.when(jnp.logical_and(more, around))
        def _():
            for m in (1, 2):
                send_around(t, m).start()

        @pl.when(jnp.logical_and(more, lax.rem(sec, 4) > 0))
        def _():
            for m in (1, 2):
                send_down(t, m).start()

        @pl.when(jnp.logical_not(more))
        def _():
            emit_last((1, 2))

    def emit_late(t, m):
        more = t < ticks - 1

        @pl.when(jnp.logical_and(more, sec > 0))
        def _():
            send_down(t, m).start()

        @pl.when(jnp.logical_not(more))
        def _():
            emit_last((m,))

    def relay(t):
        @pl.when(jnp.logical_and(t < ticks - 1, passes))
        def _():
            for m in (1, 2):
                wait_for(rbuf.at[t, m - 1], r_r.at[t, m - 1])
                pass_on(t, m).start()

    def unpack(src, dst):
        wide[...] = src[...].astype(f32)
        for r in range(2):
            dst[128 * r:128 * r + 128] = wide[pl.ds(r, C, stride=2), :].T.astype(bf16)

    def pack(src, dst):
        for r in range(2):
            wide[pl.ds(r, C, stride=2), :] = src[128 * r:128 * r + 128].astype(f32).T
        dst[...] = wide[...].astype(bf16)

    def msg_wait(t, m):
        @pl.when(jnp.logical_and(t > 0, jnp.logical_not(top)))
        def _():
            wait_for(msg.at[t, m], m_r.at[t, m])

    def take_fresh(t):
        @pl.when(jnp.logical_and(t < ticks - 1, top))
        def _():
            for m in (3, 0, 1, 2):
                wait_for(later.at[t, m], f_r.at[t + 1, m])
                unpack(later.at[t, m], msg.at[t + 1, m])

    w = lax.broadcasted_iota(jnp.int32, (128, C), 0)

    def put(f, r, v):
        V[f, 1, r] = v.astype(bf16)
        V[f, 0, r] = jnp.where(w == 0, 0.0, pltpu.roll(v, 1, 0)).astype(bf16)
        V[f, 2, r] = jnp.where(w == 127, 0.0, pltpu.roll(v, 127, 0)).astype(bf16)

    def window(f, a, b):
        return V[f, b, a:a + 2].reshape(256, C)

    hoff = pl.multiple_of(128 * (1 - c), 128)
    hrow = 3 * (1 - c)

    def halo_send(t, f, src):
        rc(src.at[pl.ds(hoff, 128), :], halo.at[t, f], h_s.at[t, f], h_r.at[t, f], CP).start()

    def halo_put(t, f):
        wait_for(halo.at[t, f], h_r.at[t, f])
        put(f, hrow, halo[t, f].astype(f32))

    def kernel_grads(k, t, fa, g):
        gt = g.T
        for a in range(3):
            for b in range(3):
                gp[k, t, 3 * a + b] = jnp.dot(
                    gt, window(fa, a, b), preferred_element_type=f32).astype(bf16)

    def conv(k, t, f):
        acc = jnp.zeros((256, C), f32)
        for a in range(3):
            for b in range(3):
                acc = acc + lax.dot_general(
                    window(f, a, b), kbuf[k, t, 3 * a + b], (((1,), (1,)), ((), ())),
                    preferred_element_type=f32)
        return acc

    def conv_flip(k, t, f):
        acc = jnp.zeros((256, C), f32)
        for a in range(3):
            for b in range(3):
                acc = acc + jnp.dot(
                    window(f, 2 - a, 2 - b), kbuf[k, t, 3 * a + b], preferred_element_type=f32)
        return acc

    par[...] = par_in[...]
    mom[...] = mom_in[...]
    gather_0(G, 0)
    for m in (3, 0, 1, 2):
        swap(inbox.at[m], first.at[m], f_s.at[0, m], f_r.at[0, m])
    V[:, :, 3 * c] = jnp.zeros((4, 3, 128, C), bf16)
    def open_first(m):
        wait_for(first.at[m], f_r.at[0, m])
        unpack(first.at[m], msg.at[0, m])

    gather_1(G, 0)
    gather_0(F, 0)

    @pl.when(top)
    def _():
        for t in range(ticks - 1):
            for m in (3, 0, 1, 2):
                swap(fresh.at[t, m], later.at[t, m], f_s.at[t + 1, m], f_r.at[t + 1, m])

    open_first(3)
    open_first(0)
    open_first(1)
    open_first(2)

    def begin(t):
        msg_wait(t, 3)
        halo_send(t, 1, msg.at[t, 3])
        msg_wait(t, 0)
        for r in range(2):
            v = msg[t, 0, 128 * r:128 * r + 128].astype(f32)
            abuf[t, 0, 128 * r:128 * r + 128] = jax.nn.silu(v).astype(bf16)
        halo_send(t, 0, abuf.at[t, 0])
        for r in range(2):
            put(0, 1 + r, abuf[t, 0, 128 * r:128 * r + 128].astype(f32))
            put(1, 1 + r, msg[t, 3, 128 * r:128 * r + 128].astype(f32))

    def grads_g(t):
        halo_put(t, 1)
        halo_put(t, 0)
        kernel_grads(G, t, 0, msg[t, 3])
        reduce_0(G, t)

    def convs_g(t):
        gather_4(G, t)
        msg_wait(t, 1)
        prev_two = (msg[t, 1].astype(f32) - conv(G, t, 0)).astype(bf16)
        obuf[t, 1] = prev_two
        abuf[t, 1] = jax.nn.silu(prev_two.astype(f32)).astype(bf16)
        halo_send(t, 2, abuf.at[t, 1])
        msg_wait(t, 2)
        back_one = (msg[t, 2].astype(f32)
                    + slope(msg[t, 0].astype(f32)) * conv_flip(G, t, 1)).astype(bf16)
        obuf[t, 2] = back_one
        halo_send(t, 3, obuf.at[t, 2])
        emit_early(t)
        for r in range(2):
            put(2, 1 + r, abuf[t, 1, 128 * r:128 * r + 128].astype(f32))
            put(3, 1 + r, obuf[t, 2, 128 * r:128 * r + 128].astype(f32))

    def grads_f(t):
        halo_put(t, 2)
        halo_put(t, 3)
        kernel_grads(F, t, 2, obuf[t, 2])
        reduce_0(F, t)

    def convs_f(t):
        gather_4(F, t)
        obuf[t, 3] = (msg[t, 3].astype(f32)
                      + slope(obuf[t, 1].astype(f32)) * conv_flip(F, t, 3)).astype(bf16)
        emit_late(t, 3)
        obuf[t, 0] = (msg[t, 0].astype(f32) - conv(F, t, 2)).astype(bf16)
        emit_late(t, 0)

    def sent(t):
        gather_sent(G, t)
        gather_sent(F, t)
        reduce_sent(G, t)
        reduce_sent(F, t)
        for f in range(4):
            wait_for(halo.at[t, f], h_s.at[t, f])

    def step(name, t):
        k = G if name[-1] == 'G' else F
        plain = {'MG': begin, 'GR': grads_g, 'CG': convs_g, 'FR': grads_f, 'CF': convs_f,
                 'RE': relay, 'FU': take_fresh, 'SE': sent}
        if name in plain:
            plain[name](t)
            return
        stage = {'A0': gather_0, 'A1': gather_1, 'A2': gather_2, 'A3': gather_3,
                 'R1': reduce_1, 'R2': reduce_2, 'R3': reduce_3, 'RZ': update}[name[:2]]
        if name[:2] in ('A0', 'A1') and name not in ORDER[:ORDER.index('C' + name[-1])]:
            @pl.when(t < ticks - 1)
            def _():
                stage(k, t + 1)
        else:
            stage(k, t)

    def tick(t, carry):
        for name in ORDER:
            step(name, t)
        return carry

    lax.fori_loop(0, ticks, tick, 0)
    for m in range(4):
        wait_for(out.at[m], o_r.at[m])

    @pl.when(jnp.logical_not(stays))
    def _():
        for m in range(4):
            wait_for(out.at[m], o_s.at[m])
            wait_for(out.at[m], f_s.at[0, m])

    @pl.when(jnp.logical_and(top, jnp.logical_not(stays)))
    def _():
        for t in range(1, ticks):
            for m in range(4):
                wait_for(out.at[m], f_s.at[t, m])

    @pl.when(passes)
    def _():
        for t in range(ticks - 1):
            for m in range(2):
                wait_for(rbuf.at[t, m], r_s.at[t, m])

    @pl.when(sec > 0)
    def _():
        for t in range(1, ticks):
            for m in range(4):
                wait_for(out.at[m], m_s.at[t, m])


def local(inbox, fresh, params, moments):
    T = fresh.shape[0] + 1
    C = inbox.shape[3]
    cells = inbox.shape[4] * inbox.shape[5]
    raw = (C * inbox.shape[4], inbox.shape[5])
    mine = inbox.reshape(4, *raw)
    later = fresh.reshape(T - 1, 4, *raw)
    shard = params.shape[1:]
    vmem = pl.BlockSpec(memory_space=pltpu.VMEM)
    dma = pltpu.SemaphoreType.DMA
    out, par, mom, grad = pl.pallas_call(
        kernel,
        out_shape=(jax.ShapeDtypeStruct((4, *raw), bf16),) + (jax.ShapeDtypeStruct(shard, f32),) * 3,
        in_specs=[vmem, pl.BlockSpec(memory_space=pl.ANY), vmem, vmem],
        out_specs=(vmem,) * 4,
        scratch_shapes=[
            pltpu.VMEM((T, 4, cells, C), bf16),
            pltpu.VMEM((T, 4, cells, C), bf16),
            pltpu.VMEM((T, 2, cells, C), bf16),
            pltpu.VMEM((T - 1, 2, cells, C), bf16),
            pltpu.VMEM((T, 4, 128, C), bf16),
            pltpu.VMEM((4, 3, 4, 128, C), bf16),
            pltpu.VMEM((2, T, 9, C, C), bf16),
            pltpu.VMEM((2, T, 9, C // 2, C), bf16),
            pltpu.VMEM((2, T, 7, 9, 16, C), bf16),
            pltpu.VMEM((2, 9, 16, C), f32),
            pltpu.VMEM((2, T, 9, C, C), bf16),
            pltpu.VMEM((4, *raw), bf16),
            pltpu.VMEM((T - 1, 4, *raw), bf16),
            pltpu.VMEM((4, *raw), bf16),
            pltpu.VMEM(raw, f32),
            dma((2, T, 15)), dma((2, T, 15)),
            dma((2, T, 11)), dma((2, T, 11)),
            dma((T, 4)), dma((T, 4)), dma((T, 4)), dma((T, 4)), dma((T - 1, 2)), dma((T - 1, 2)),
            dma((T, 4)), dma((T, 4)),
            dma((4,)), dma((4,)),
        ],
        compiler_params=pltpu.CompilerParams(
            collective_id=0, has_side_effects=True, vmem_limit_bytes=60 << 20),
        cost_estimate=pl.CostEstimate(
            flops=T * 6 * 9 * 2 * C * C * cells, bytes_accessed=1 << 22, transcendentals=0),
        name="relay",
    )(mine, later, params[0], moments[0])
    mom = MOMENTUM * mom + grad / math.sqrt(9 * C)
    par = par - LEARN_RATE * mom
    return (out.reshape(inbox.shape), par[None], mom[None])


def solution(mesh):
    cells = P("section", None, "dp", None, "spatial", None)
    shards = P("section", None, None, ("dp", "spatial"), None)
    return jax.shard_map(
        local,
        mesh=mesh,
        in_specs=(cells, P(None, None, "dp", None, "spatial", None), shards, shards),
        out_specs=(cells, shards, shards),
        check_vma=False,
    )
```

```python
import math

import jax
import jax.numpy as jnp
from jax import lax
from jax.experimental import pallas as pl
from jax.experimental.pallas import tpu as pltpu
from jax.sharding import PartitionSpec as P

MESH = pl.DeviceIdType.MESH
LEARN_RATE = 0.05
MOMENTUM = 0.9
F, G = 0, 1
RS = ('xf', 'zf')
AG = ('dz', 'dz')
ORDER = ('MG', 'GR', 'A1F', 'A2G', 'R1G', 'A3G', 'CG', 'A2F', 'FR', 'R2G', 'R1F', 'A3F', 'RZG', 'A0G',
         'RE', 'CF', 'SB', 'R2F', 'A1G', 'FU', 'RZF', 'A0F', 'SE')
bf16, f32 = jnp.bfloat16, jnp.float32


def wait_for(ref, sem):
    pltpu.make_async_copy(ref, ref, sem).wait()


def slope(v):
    s = jax.nn.sigmoid(v)
    return s * (1.0 + v * (1.0 - s))


def kernel(inbox, fresh, par_in, mom_in, out, par, mom, last,
           msg, obuf, abuf, rbuf, halo, V, gp, crecv, mrecv, fs, kbuf, first, later, final, wide,
           ag_s, ag_r, rs_s, rs_r, m_s, m_r, f_s, f_r, r_s, r_r, h_s, h_r, o_s, o_r):
    ticks = msg.shape[0]
    C = msg.shape[3]
    scale = 1.0 / math.sqrt(9 * C)
    sec = lax.axis_index("section")
    n_sec = lax.axis_size("section")
    dp = lax.axis_index("dp")
    z = lax.axis_index("spatial")
    x = dp // 2
    c = lax.rem(dp, 2)
    xp, xm, x2 = lax.rem(x + 1, 4), lax.rem(x + 3, 4), lax.rem(x + 2, 4)
    XP = {"dp": lax.rem(dp + 2, 8)}
    XM = {"dp": lax.rem(dp + 6, 8)}
    X2 = {"dp": lax.rem(dp + 4, 8)}
    CP = {"dp": dp + 1 - 2 * c}
    ZP = {"spatial": 1 - z}
    DG = {"dp": dp + 1 - 2 * c, "spatial": 1 - z}
    def far(dev):
        return {**dev, "spatial": 1 - z}

    def at(offset):
        return {"section": lax.rem(sec + n_sec + offset, n_sec)}

    around = jnp.logical_and(lax.rem(sec, 4) == 0, sec > 0)
    passes = jnp.logical_and(lax.rem(sec, 4) == 3, sec > 3)
    top = sec == n_sec - 1
    stays = c == z

    def rc(src, dst, ss, rs, dev):
        return pltpu.make_async_remote_copy(
            src_ref=src, dst_ref=dst, send_sem=ss, recv_sem=rs,
            device_id=dev, device_id_type=MESH)

    barrier = pltpu.get_barrier_semaphore()
    for dev in (XP, XM, X2, CP, ZP, DG, at(1), at(-1), at(3), at(-3), at(4), at(-4)):
        pl.semaphore_signal(barrier, inc=1, device_id=dev, device_id_type=MESH)
    pl.semaphore_wait(barrier, 12)

    def row(xx, cc, zz):
        return pl.multiple_of(64 * xx + 32 * cc + 16 * zz, 16)

    def kpart(k, t, xx, zz):
        return kbuf.at[k, t, :, pl.ds(row(xx, c, zz), 16), :]

    def ag(k, t, i, xx, zz, dev):
        part = kpart(k, t, xx, zz)
        return rc(part, part, ag_s.at[k, t, i], ag_r.at[k, t, i], dev)

    def ag_to(k, t, zz):
        ways = [ag(k, t, 5 + zz, x, zz, XP), ag(k, t, 1 + zz, x, zz, XM)]
        if AG[k] == 'dz':
            ways.append(ag(k, t, 3 + zz, x, zz, X2))
        return ways + [ag(k, t, 13 + zz, x, zz, CP)]

    def ag_wait(k, t, i):
        wait_for(kpart(k, t, x, z), ag_r.at[k, t, i])

    def gather_0(k, t):
        kbuf[k, t, :, pl.ds(row(x, c, z), 16), :] = (par[k] * scale).astype(bf16)
        ag(k, t, 0, x, z, ZP).start()
        for d in ag_to(k, t, z):
            d.start()

    def gather_1(k, t):
        ag_wait(k, t, 0)
        for d in ag_to(k, t, 1 - z):
            d.start()

    def hand_over(k, t, zz):
        for d, xx in ((0, xp), (2, xm), (1, x2)):
            ag_wait(k, t, 1 + 2 * d + zz)
            ag(k, t, 7 + 2 * d + zz, xx, zz, CP).start()

    def gather_2(k, t):
        if AG[k] == 'dz':
            hand_over(k, t, z)
            return
        ag_wait(k, t, 5)
        ag(k, t, 3, xm, 0, XP).start()
        ag(k, t, 11, xm, 0, CP).start()
        ag_wait(k, t, 2)
        ag(k, t, 4, xp, 1, XM).start()
        ag(k, t, 8, xp, 1, CP).start()
        ag_wait(k, t, 6)
        ag(k, t, 12, xm, 1, CP).start()
        ag_wait(k, t, 1)
        ag(k, t, 7, xp, 0, CP).start()

    def gather_3(k, t):
        if AG[k] == 'dz':
            hand_over(k, t, 1 - z)
            return
        for zz in range(2):
            ag_wait(k, t, 3 + zz)
            ag(k, t, 9 + zz, x2, zz, CP).start()

    def gather_4(k, t):
        for i in range(7, 15):
            ag_wait(k, t, i)

    def gather_sent(k, t):
        for i in range(15):
            wait_for(kpart(k, t, x, z), ag_s.at[k, t, i])

    def gpart(k, t, xx, zz):
        return gp.at[k, t, :, pl.ds(row(xx, c, zz), 16), :]

    order = (x2, xp, xm, x)

    def reduce_0(k, t):
        for j in range(4):
            rc(gp.at[k, t, :, pl.ds(row(order[j], 1 - c, 0), 32), :],
               crecv.at[k, t, :, pl.ds(pl.multiple_of(32 * order[j], 32), 32), :],
               rs_s.at[k, t, j], rs_r.at[k, t, j], CP).start()

    def part_to(k, t, m, xx, zz, dev):
        return rc(gpart(k, t, xx, zz), mrecv.at[k, t, m], rs_s.at[k, t, 4 + m], rs_r.at[k, t, 4 + m], dev)

    def part_wait(k, t, m):
        wait_for(mrecv.at[k, t, m], rs_r.at[k, t, 4 + m])

    def part_add(k, t, m, xx, zz):
        part_wait(k, t, m)
        mine = gpart(k, t, xx, zz)
        mine[...] = (mine[...].astype(f32) + mrecv[k, t, m].astype(f32)).astype(bf16)

    def reduce_1(k, t):
        for j in range(4):
            xx = order[j]
            other = crecv.at[k, t, :, pl.ds(pl.multiple_of(32 * xx, 32), 32), :]
            wait_for(other, rs_r.at[k, t, j])
            mine = gp.at[k, t, :, pl.ds(row(xx, c, 0), 32), :]
            mine[...] = (mine[...].astype(f32) + other[...].astype(f32)).astype(bf16)
            dev = (X2, XP, XM, None)[j]
            m = (2, 0, 1, 6)[j]
            if RS[k] == 'zf':
                part_to(k, t, j, xx, 1 - z, ZP).start()
            elif RS[k] == 'xf':
                for zz in range(2):
                    if j < 3:
                        part_to(k, t, 2 * j + zz, xx, zz, dev).start()
            elif RS[k] == 'cur':
                if j == 0:
                    part_to(k, t, 0, xx, 0, XP).start()
                    part_to(k, t, 3, xx, 1, XM).start()
                elif j == 1:
                    part_to(k, t, 1, xx, 1, XP).start()
                elif j == 2:
                    part_to(k, t, 4, xx, 0, XM).start()
            elif dev is None:
                part_to(k, t, 6, xx, 1 - z, ZP).start()
            else:
                part_to(k, t, m + 3, xx, 1 - z, far(dev)).start()
                part_to(k, t, m, xx, z, dev).start()

    def reduce_2(k, t):
        if RS[k] == 'zf':
            for j in range(4):
                part_add(k, t, j, order[j], z)
                if j < 3:
                    part_to(k, t, 4 + j, order[j], z, (X2, XP, XM)[j]).start()
        if RS[k] == 'cur':
            part_add(k, t, 0, xp, 0)
            part_to(k, t, 2, xp, 0, XP).start()
            part_add(k, t, 3, xm, 1)
            part_to(k, t, 5, xm, 1, XM).start()

        if RS[k] == 'xf':
            for m in (2, 3, 4, 5, 0, 1):
                part_wait(k, t, m)

            def total(zz):
                grad = gpart(k, t, x, zz)[...].astype(f32)
                for j in range(3):
                    grad = grad + mrecv[k, t, 2 * j + zz].astype(f32)
                return grad

            theirs = gpart(k, t, x, 1 - z)
            theirs[...] = total(1 - z).astype(bf16)
            part_to(k, t, 6, x, 1 - z, ZP).start()
            fs[k] = total(z)

    def reduce_3(k, t):
        if RS[k] == 'cur':
            for m in (1, 4, 2, 5):
                part_wait(k, t, m)

            def total(zz):
                return (gpart(k, t, x, zz)[...].astype(f32)
                        + mrecv[k, t, 2 - zz].astype(f32) + mrecv[k, t, 4 + zz].astype(f32))

            theirs = gpart(k, t, x, 1 - z)
            theirs[...] = total(1 - z).astype(bf16)
            part_to(k, t, 6, x, 1 - z, ZP).start()
            fs[k] = total(z)

    def update(k, t):
        late = {'zf': (4, 5, 6), 'cur': (6,), 'xf': (6,), 'direct': range(7)}[RS[k]]
        grad = fs[k] if RS[k] in ('cur', 'xf') else gpart(k, t, x, z)[...].astype(f32)
        for m in late:
            part_wait(k, t, m)
        for m in late:
            grad = grad + mrecv[k, t, m].astype(f32)
        @pl.when(t < ticks - 1)
        def _():
            mom[k] = MOMENTUM * mom[k] + scale * grad
            par[k] = par[k] - LEARN_RATE * mom[k]

        @pl.when(t == ticks - 1)
        def _():
            last[k] = grad

    def reduce_sent(k, t):
        for j in range(4):
            wait_for(crecv.at[k, t, :, pl.ds(0, 32), :], rs_s.at[k, t, j])
        for i in range(4, 11):
            wait_for(mrecv.at[k, t, 0], rs_s.at[k, t, i])

    def swap(src, dst, ss, rs):
        @pl.when(stays)
        def _():
            pltpu.make_async_copy(src, dst, rs).start()

        @pl.when(jnp.logical_not(stays))
        def _():
            rc(src, dst, ss, rs, DG).start()

    def send_down(t, m):
        return rc(obuf.at[t, m], msg.at[t + 1, m], m_s.at[t + 1, m], m_r.at[t + 1, m], at(-1))

    def send_around(t, m):
        return rc(obuf.at[t, m], rbuf.at[t, m - 1], m_s.at[t + 1, m], r_r.at[t, m - 1], at(3))

    def pass_on(t, m):
        return rc(rbuf.at[t, m - 1], msg.at[t + 1, m], r_s.at[t, m - 1], m_r.at[t + 1, m], at(-4))

    def emit_last(members):
        for m in members:
            pack(obuf.at[ticks - 1, m], final.at[m])
            swap(final.at[m], out.at[m], o_s.at[m], o_r.at[m])

    def emit_early(t):
        more = t < ticks - 1

        @pl.when(jnp.logical_and(more, around))
        def _():
            for m in (1, 2):
                send_around(t, m).start()

        @pl.when(jnp.logical_and(more, lax.rem(sec, 4) > 0))
        def _():
            for m in (1, 2):
                send_down(t, m).start()

        @pl.when(jnp.logical_not(more))
        def _():
            emit_last((1, 2))

    def emit_late(t, m):
        more = t < ticks - 1

        @pl.when(jnp.logical_and(more, sec > 0))
        def _():
            send_down(t, m).start()

        @pl.when(jnp.logical_not(more))
        def _():
            emit_last((m,))

    def relay(t):
        @pl.when(jnp.logical_and(t < ticks - 1, passes))
        def _():
            for m in (1, 2):
                wait_for(rbuf.at[t, m - 1], r_r.at[t, m - 1])
                pass_on(t, m).start()

    def unpack(src, dst):
        wide[...] = src[...].astype(f32)
        for r in range(2):
            dst[128 * r:128 * r + 128] = wide[pl.ds(r, C, stride=2), :].T.astype(bf16)

    def pack(src, dst):
        for r in range(2):
            wide[pl.ds(r, C, stride=2), :] = src[128 * r:128 * r + 128].astype(f32).T
        dst[...] = wide[...].astype(bf16)

    def msg_wait(t, m):
        @pl.when(jnp.logical_and(t > 0, jnp.logical_not(top)))
        def _():
            wait_for(msg.at[t, m], m_r.at[t, m])

    def take_fresh(t):
        @pl.when(jnp.logical_and(t < ticks - 1, top))
        def _():
            for m in (3, 0, 1, 2):
                wait_for(later.at[t, m], f_r.at[t + 1, m])
                unpack(later.at[t, m], msg.at[t + 1, m])

    w = lax.broadcasted_iota(jnp.int32, (128, C), 0)

    def put(f, r, v):
        V[f, 1, r] = v.astype(bf16)
        V[f, 0, r] = jnp.where(w == 0, 0.0, pltpu.roll(v, 1, 0)).astype(bf16)
        V[f, 2, r] = jnp.where(w == 127, 0.0, pltpu.roll(v, 127, 0)).astype(bf16)

    def window(f, a, b):
        return V[f, b, a:a + 2].reshape(256, C)

    hoff = pl.multiple_of(128 * (1 - c), 128)
    hrow = 3 * (1 - c)

    def halo_send(t, f, src):
        rc(src.at[pl.ds(hoff, 128), :], halo.at[t, f], h_s.at[t, f], h_r.at[t, f], CP).start()

    def halo_put(t, f):
        wait_for(halo.at[t, f], h_r.at[t, f])
        put(f, hrow, halo[t, f].astype(f32))

    def kernel_grads(k, t, fa, g):
        gt = g.T
        for a in range(3):
            for b in range(3):
                gp[k, t, 3 * a + b] = jnp.dot(
                    gt, window(fa, a, b), preferred_element_type=f32).astype(bf16)

    def conv(k, t, f):
        acc = jnp.zeros((256, C), f32)
        for a in range(3):
            for b in range(3):
                acc = acc + lax.dot_general(
                    window(f, a, b), kbuf[k, t, 3 * a + b], (((1,), (1,)), ((), ())),
                    preferred_element_type=f32)
        return acc

    def conv_flip(k, t, f):
        acc = jnp.zeros((256, C), f32)
        for a in range(3):
            for b in range(3):
                acc = acc + jnp.dot(
                    window(f, 2 - a, 2 - b), kbuf[k, t, 3 * a + b], preferred_element_type=f32)
        return acc

    par[...] = par_in[...]
    mom[...] = mom_in[...]
    gather_0(G, 0)
    for m in (3, 0, 1, 2):
        swap(inbox.at[m], first.at[m], f_s.at[0, m], f_r.at[0, m])
    V[:, :, 3 * c] = jnp.zeros((4, 3, 128, C), bf16)
    def open_first(m):
        wait_for(first.at[m], f_r.at[0, m])
        unpack(first.at[m], msg.at[0, m])

    gather_1(G, 0)
    gather_0(F, 0)

    @pl.when(top)
    def _():
        for t in range(ticks - 1):
            for m in (3, 0, 1, 2):
                swap(fresh.at[t, m], later.at[t, m], f_s.at[t + 1, m], f_r.at[t + 1, m])

    open_first(3)
    open_first(0)
    open_first(1)
    open_first(2)

    def begin(t):
        msg_wait(t, 3)
        halo_send(t, 1, msg.at[t, 3])
        msg_wait(t, 0)
        for r in range(2):
            v = msg[t, 0, 128 * r:128 * r + 128].astype(f32)
            abuf[t, 0, 128 * r:128 * r + 128] = jax.nn.silu(v).astype(bf16)
        halo_send(t, 0, abuf.at[t, 0])
        for r in range(2):
            put(0, 1 + r, abuf[t, 0, 128 * r:128 * r + 128].astype(f32))
            put(1, 1 + r, msg[t, 3, 128 * r:128 * r + 128].astype(f32))

    def grads_g(t):
        halo_put(t, 1)
        halo_put(t, 0)
        kernel_grads(G, t, 0, msg[t, 3])
        reduce_0(G, t)

    def convs_g(t):
        gather_4(G, t)
        msg_wait(t, 1)
        prev_two = (msg[t, 1].astype(f32) - conv(G, t, 0)).astype(bf16)
        obuf[t, 1] = prev_two
        abuf[t, 1] = jax.nn.silu(prev_two.astype(f32)).astype(bf16)
        halo_send(t, 2, abuf.at[t, 1])
        msg_wait(t, 2)
        back_one = (msg[t, 2].astype(f32)
                    + slope(msg[t, 0].astype(f32)) * conv_flip(G, t, 1)).astype(bf16)
        obuf[t, 2] = back_one
        halo_send(t, 3, obuf.at[t, 2])
        emit_early(t)
        for r in range(2):
            put(2, 1 + r, abuf[t, 1, 128 * r:128 * r + 128].astype(f32))
            put(3, 1 + r, obuf[t, 2, 128 * r:128 * r + 128].astype(f32))

    def grads_f(t):
        halo_put(t, 2)
        halo_put(t, 3)
        kernel_grads(F, t, 2, obuf[t, 2])
        reduce_0(F, t)

    def convs_f(t):
        gather_4(F, t)
        obuf[t, 3] = (msg[t, 3].astype(f32)
                      + slope(obuf[t, 1].astype(f32)) * conv_flip(F, t, 3)).astype(bf16)
        emit_late(t, 3)
        obuf[t, 0] = (msg[t, 0].astype(f32) - conv(F, t, 2)).astype(bf16)
        emit_late(t, 0)

    def sent_before(t):
        gather_sent(G, t)
        gather_sent(F, t)
        reduce_sent(G, t)
        for f in range(4):
            wait_for(halo.at[t, f], h_s.at[t, f])

    def sent(t):
        reduce_sent(F, t)

    def step(name, t):
        k = G if name[-1] == 'G' else F
        plain = {'MG': begin, 'GR': grads_g, 'CG': convs_g, 'FR': grads_f, 'CF': convs_f,
                 'RE': relay, 'FU': take_fresh, 'SE': sent, 'SB': sent_before}
        if name in plain:
            plain[name](t)
            return
        stage = {'A0': gather_0, 'A1': gather_1, 'A2': gather_2, 'A3': gather_3,
                 'R1': reduce_1, 'R2': reduce_2, 'R3': reduce_3, 'RZ': update}[name[:2]]
        if name[:2] in ('A0', 'A1') and name not in ORDER[:ORDER.index('C' + name[-1])]:
            @pl.when(t < ticks - 1)
            def _():
                stage(k, t + 1)
        else:
            stage(k, t)

    def tick(t, carry):
        for name in ORDER:
            step(name, t)
        return carry

    lax.fori_loop(0, ticks, tick, 0)
    for m in range(4):
        wait_for(out.at[m], o_r.at[m])

    @pl.when(jnp.logical_not(stays))
    def _():
        for m in range(4):
            wait_for(out.at[m], o_s.at[m])
            wait_for(out.at[m], f_s.at[0, m])

    @pl.when(jnp.logical_and(top, jnp.logical_not(stays)))
    def _():
        for t in range(1, ticks):
            for m in range(4):
                wait_for(out.at[m], f_s.at[t, m])

    @pl.when(passes)
    def _():
        for t in range(ticks - 1):
            for m in range(2):
                wait_for(rbuf.at[t, m], r_s.at[t, m])

    @pl.when(sec > 0)
    def _():
        for t in range(1, ticks):
            for m in range(4):
                wait_for(out.at[m], m_s.at[t, m])


def local(inbox, fresh, params, moments):
    T = fresh.shape[0] + 1
    C = inbox.shape[3]
    cells = inbox.shape[4] * inbox.shape[5]
    raw = (C * inbox.shape[4], inbox.shape[5])
    mine = inbox.reshape(4, *raw)
    later = fresh.reshape(T - 1, 4, *raw)
    shard = params.shape[1:]
    vmem = pl.BlockSpec(memory_space=pltpu.VMEM)
    dma = pltpu.SemaphoreType.DMA
    out, par, mom, grad = pl.pallas_call(
        kernel,
        out_shape=(jax.ShapeDtypeStruct((4, *raw), bf16),) + (jax.ShapeDtypeStruct(shard, f32),) * 3,
        in_specs=[vmem, pl.BlockSpec(memory_space=pl.ANY), vmem, vmem],
        out_specs=(vmem,) * 4,
        scratch_shapes=[
            pltpu.VMEM((T, 4, cells, C), bf16),
            pltpu.VMEM((T, 4, cells, C), bf16),
            pltpu.VMEM((T, 2, cells, C), bf16),
            pltpu.VMEM((T - 1, 2, cells, C), bf16),
            pltpu.VMEM((T, 4, 128, C), bf16),
            pltpu.VMEM((4, 3, 4, 128, C), bf16),
            pltpu.VMEM((2, T, 9, C, C), bf16),
            pltpu.VMEM((2, T, 9, C // 2, C), bf16),
            pltpu.VMEM((2, T, 7, 9, 16, C), bf16),
            pltpu.VMEM((2, 9, 16, C), f32),
            pltpu.VMEM((2, T, 9, C, C), bf16),
            pltpu.VMEM((4, *raw), bf16),
            pltpu.VMEM((T - 1, 4, *raw), bf16),
            pltpu.VMEM((4, *raw), bf16),
            pltpu.VMEM(raw, f32),
            dma((2, T, 15)), dma((2, T, 15)),
            dma((2, T, 11)), dma((2, T, 11)),
            dma((T, 4)), dma((T, 4)), dma((T, 4)), dma((T, 4)), dma((T - 1, 2)), dma((T - 1, 2)),
            dma((T, 4)), dma((T, 4)),
            dma((4,)), dma((4,)),
        ],
        compiler_params=pltpu.CompilerParams(
            collective_id=0, has_side_effects=True, vmem_limit_bytes=60 << 20),
        cost_estimate=pl.CostEstimate(
            flops=T * 6 * 9 * 2 * C * C * cells, bytes_accessed=1 << 22, transcendentals=0),
        name="relay",
    )(mine, later, params[0], moments[0])
    mom = MOMENTUM * mom + grad / math.sqrt(9 * C)
    par = par - LEARN_RATE * mom
    return (out.reshape(inbox.shape), par[None], mom[None])


def solution(mesh):
    cells = P("section", None, "dp", None, "spatial", None)
    shards = P("section", None, None, ("dp", "spatial"), None)
    return jax.shard_map(
        local,
        mesh=mesh,
        in_specs=(cells, P(None, None, "dp", None, "spatial", None), shards, shards),
        out_specs=(cells, shards, shards),
        check_vma=False,
    )
```
